32 devices in a mesh: owner: 4 (over y, x), batch: 8 (over z, core).
Axes of the slice: x: 2, y: 2, z: 4, core: 2. Of those that a mesh axis runs over, the one named last changes fastest.
Arguments:
- hidden: bfloat16 [512, 6144], P(('owner', 'batch')), may hold values from -6 to 6
- gains: float32 [2, 6144], replicated, may hold values from 0.25 to 1.75
- up_rows: bfloat16 [98304, 6144], P(('owner', 'batch')), may hold values from -0.078125 to 0.078125
- down_rows: bfloat16 [98304, 6144], P(('owner', 'batch')), may hold values from -0.1875 to 0.1875
- pick: int32 [4, 32], replicated, may hold values from 0 to 24, as said below
Outputs:
- final_rows: bfloat16 [512, 6144], P(('owner', 'batch'))
The draws below stay inside these ranges and needn't reach their ends.
Inputs may be any that keep to these rules, and one draw needn't show every extreme that they name: pick[g, u] names the one block among unit u's 24 blocks that row block g uses, or is 24 when it uses none of them. In every row block there is a lane of which every unit is used, and a unit that is not.
All inputs are finite; a program needn't handle non-finite values.
Results may differ from the reference program's by a relative error of at most 0.018.
Values may be sent and summed in bfloat16 or wider, within the bound.
A program may use at most 192 MiB of HBM per device.

```python
import jax
import jax.numpy as jnp
from jax import lax

D = 6144
FF = 49152
BLOCK = 128
LAYERS = 2
HELD = 24
GROUP_ROWS = 128
REQUESTS = 512
N_OWNER = 4
N_BATCH = 8
DEVICES = 32


def draw_pick(key, part):
    keys = jax.random.split(jax.random.fold_in(key, 17), 5)
    level = jax.random.randint(keys[0], (N_OWNER, 1), 1, 10)
    roll = jax.random.randint(keys[1], (N_OWNER, DEVICES), 0, 10)
    which = jax.random.randint(keys[2], (N_OWNER, DEVICES), 0, HELD)
    chosen = jnp.where(roll < level, which, HELD)
    unit_ids = jnp.arange(DEVICES)[None, :]
    full_lane = jax.random.randint(keys[3], (N_OWNER, 1), 0, N_BATCH)
    chosen = jnp.where(unit_ids % N_BATCH == full_lane, which, chosen)
    empty_lane = (full_lane + 1 + jax.random.randint(keys[4], (N_OWNER, 1), 0, N_BATCH - 1)) % N_BATCH
    chosen = jnp.where(unit_ids == empty_lane, HELD, chosen)
    return chosen.astype(jnp.int32)


def level_of(stream_key, shape, cuts, least, largest):
    gain, own = 1.0, jax.random.fold_in(stream_key, 6)
    for dim, parts in cuts:
        heights = jnp.exp(jax.random.uniform(jax.random.fold_in(own, dim), (parts,), jnp.float32, least / len(cuts), largest / len(cuts)))
        gain = gain * jnp.repeat(heights, shape[dim] // parts).reshape([-1 if axis == dim else 1 for axis in range(len(shape))])
    return gain


def bell_draw(own_key, dims, scale, most, cuts=(), dtype=jnp.bfloat16):
    level = level_of(own_key, dims, cuts, -0.22, 0.18) if cuts else 1.0
    entries = jax.random.normal(own_key, dims, jnp.float32) * scale * level
    return jnp.minimum(jnp.maximum(entries, -most), most).astype(dtype)


def setup_inputs(seed: int = 0) -> dict:
    key_list = jax.random.split(jax.random.key(seed), 6)
    hidden = bell_draw(key_list[0], (REQUESTS, D), 1.0, 6.0, ((0, 32),))
    gains = jnp.clip(1.0 + 0.15 * jax.random.normal(key_list[1], (LAYERS, D), jnp.float32), 0.25, 1.75)
    up_rows = bell_draw(key_list[2], (LAYERS * FF, D), D ** -0.5, 0.078125, ((0, 32),))
    down_rows = bell_draw(key_list[3], (LAYERS * FF, D), (DEVICES * BLOCK // 4) ** -0.5, 0.1875, ((0, 32),))
    pick = draw_pick(jax.random.fold_in(key_list[5], 71), 0)
    return {"hidden": hidden, "gains": gains, "up_rows": up_rows, "down_rows": down_rows, "pick": pick}


def normalize(rows_in, gain_row):
    values = rows_in.astype(jnp.float32)
    row_mean = lax.optimization_barrier(jnp.mean(values, axis=1, keepdims=True))
    centered = values - row_mean
    row_var = lax.optimization_barrier(jnp.mean(centered * centered, axis=1, keepdims=True))
    return (centered * lax.rsqrt(row_var + 1e-05) * gain_row[None, :]).astype(jnp.bfloat16)

def reference(hidden, gains, up_rows, down_rows, pick):
    dev_layer = DEVICES // LAYERS
    up_stack = up_rows.reshape(DEVICES * HELD, BLOCK, D)
    down_stack = down_rows.reshape(DEVICES * HELD, BLOCK, D)
    state = hidden
    for layer_at in range(LAYERS):
        normed = normalize(state, gains[layer_at])
        pieces = []
        for group_at in range(N_OWNER):
            units = (layer_at * dev_layer + jnp.arange(dev_layer)).astype(jnp.int32)
            chosen = pick[group_at, units]
            live_units = (chosen < HELD).astype(jnp.float32)
            selected = (units * HELD + jnp.minimum(chosen, HELD - 1)).astype(jnp.int32)
            up_sel = up_stack[selected].reshape(dev_layer * BLOCK, D)
            down_sel = down_stack[selected].astype(jnp.float32)
            group_rows = normed[group_at * GROUP_ROWS:(group_at + 1) * GROUP_ROWS]
            pre_act = jnp.dot(group_rows, up_sel.T, preferred_element_type=jnp.float32)
            neuron_mask = jnp.repeat(live_units, BLOCK)
            active = (jnp.maximum(pre_act, 0.0) * neuron_mask[None, :]).astype(jnp.bfloat16)
            active_four = active.astype(jnp.float32).reshape(GROUP_ROWS, dev_layer // N_BATCH, N_BATCH, BLOCK)
            down_four = down_sel.reshape(dev_layer // N_BATCH, N_BATCH, BLOCK, D)
            lane_terms = jnp.einsum('rjbk,jbkd->brd', active_four, down_four)
            lane_sum = lax.optimization_barrier(lane_terms.astype(jnp.bfloat16))
            pieces.append(lax.optimization_barrier(jnp.sum(lane_sum.astype(jnp.float32), axis=0)))
        update = jnp.concatenate(pieces, axis=0)
        state = (state.astype(jnp.float32) + update).astype(jnp.bfloat16)
    return state
```

```python
import functools

import jax
import jax.numpy as jnp
from jax import lax
from jax.experimental import pallas as pl
from jax.experimental.pallas import tpu as pltpu
from jax.sharding import PartitionSpec as P

BLOCK = 128
LAYERS = 2
CORES = 2
TWINS = 2
VMEM_BUDGET = 60 * 1024 * 1024
CHUNK = 1024


def sublayers_kernel(
    owners, batches,
    hidden_ref, gains_ref, live_ref, up_hbm, down_hbm, out_ref,
    state, acts, up_v, down_v, pre, pre_in, part, x_in, y_in, q_in, z_in, r_in, stat, stat_in, out_in, total,
    wsem, hsem, osem, ssem, pre_sem, ag_recv, x_send, y_send, up_send, dn_send,
    rx_send, ry_send, rup_send, rdn_send, x_recv, y_recv, q_recv, z_recv, r_recv,
):
    zn = batches // CORES
    per_layer = owners // LAYERS
    rows, width = hidden_ref.shape
    half = width // CORES
    group_rows = batches * rows
    me_o = lax.axis_index("owner")
    me_b = lax.axis_index("batch")
    hi, lo = me_o // per_layer, me_o % per_layer
    zi, core = me_b // CORES, me_b % CORES
    peer_x = hi * per_layer + (1 - lo)
    peer_y = (1 - hi) * per_layer + lo
    diag = (1 - hi) * per_layer + (1 - lo)
    x_dev, y_dev = (peer_x, me_b), (peer_y, me_b)
    p_dev = (me_o, zi * CORES + 1 - core)
    up_dev, dn_dev = (me_o, me_b + CORES), (me_o, me_b - CORES)
    has_up, has_dn = zi < zn - 1, zi > 0
    lower = zi < zn // 2
    upper = zi >= zn // 2
    low = lower.astype(jnp.int32)
    twin = zi + 1 - 2 * (zi % 2)
    inner = jnp.logical_and(zi > 0, zi < zn - 1)
    inner_lower, inner_upper = jnp.logical_and(inner, lower), jnp.logical_and(inner, upper)
    mine = pl.ds(pl.multiple_of(core * half, 128), half)
    theirs = pl.ds(pl.multiple_of((1 - core) * half, 128), half)
    parts = range(CORES)

    def remote(src, dst, send, recv, dev):
        return pltpu.make_async_remote_copy(
            src_ref=src, dst_ref=dst, send_sem=send, recv_sem=recv,
            device_id=dev, device_id_type=pl.DeviceIdType.MESH)

    def always():
        return True

    def when(cond, run):
        if cond is True:
            run()
        else:
            pl.when(cond)(run)

    barrier = pltpu.get_barrier_semaphore()
    for cond, dev in ((True, x_dev), (True, y_dev), (True, p_dev), (has_up, up_dev), (has_dn, dn_dev)):
        when(cond, lambda dev=dev: pl.semaphore_signal(
            barrier, inc=1, device_id=dev, device_id_type=pl.DeviceIdType.MESH))
    pl.semaphore_wait(barrier, 3 + has_up.astype(jnp.int32) + has_dn.astype(jnp.int32))

    swap = remote(hidden_ref.at[:, theirs], state.at[core], hsem.at[0], hsem.at[1], p_dev)
    swap.start()

    blocks = ((up_hbm, up_v), (down_hbm, down_v))

    def keep(n, g):
        hbm, vmem = blocks[n]
        return pltpu.make_async_copy(hbm.at[g, :, mine], vmem.at[g, core], wsem.at[n, 0, g])

    def give(n, g):
        hbm, vmem = blocks[n]
        return remote(hbm.at[g, :, theirs], vmem.at[g, core], wsem.at[n, 1, g], wsem.at[n, 2, g], p_dev)

    for n in range(len(blocks)):
        for g in range(owners):
            keep(n, g).start()
            give(n, g).start()
    state[core] = hidden_ref[:, mine]
    swap.wait()

    def wait_weight(n, g):
        keep(n, g).wait()
        give(n, g).wait_recv()

    class Sender:
        def __init__(self, layer):
            self.layer, self.log = layer, []

        def go(self, src, dst, send, recv, dev, cond=always):
            when(cond(), lambda: remote(src, dst, send(self.layer), recv, dev).start())
            self.log.append((send, cond))

        def spread_piece(self, sems, g, j, i, slot, dev, cond):
            ref = acts.at[self.layer, g, j, i]
            self.go(ref, ref, lambda layer: sems.at[layer, slot, i], ag_recv.at[self.layer, g, j, i], dev, cond)

        def x(self, g, j, i, slot, cond=always):
            self.spread_piece(x_send, g, j, i, slot, x_dev, cond)

        def y(self, g, j, i, slot, cond=always):
            self.spread_piece(y_send, g, j, i, slot, y_dev, cond)

        def up(self, g, j, i, slot, cond):
            self.spread_piece(up_send, g, j, i, slot, up_dev, cond)

        def dn(self, g, j, i, slot, cond):
            self.spread_piece(dn_send, g, j, i, slot, dn_dev, cond)

    def arrive(layer, g, j, i):
        ref = acts.at[layer, g, j, i]
        remote(ref, ref, x_send.at[0, 0, 0], ag_recv.at[layer, g, j, i], x_dev).wait_recv()

    def below(k):
        return lambda: zi - k >= 0

    def above(k):
        return lambda: zi + k < zn

    def column(t, k, i, onward):
        for j, there, slot, send, more in (
            (zi - k, below(k), k, t.up, has_up), (zi + k, above(k), zn - 1 + k, t.dn, has_dn),
        ):
            when(there(), lambda j=j: arrive(t.layer, me_o, j, i))
            if k < zn - 1:
                send(me_o, j, i, k, lambda there=there, more=more: jnp.logical_and(there(), more))
            onward(j, there, slot)

    def combine(dst, terms):
        total = dst[...].astype(jnp.float32)
        for term in terms:
            total = total + term[...].astype(jnp.float32)
        dst[...] = total.astype(jnp.bfloat16)

    def line(t, col, k, i, fold):
        for j, there, slot, behind, sends, dev in (
            (zi + k, above(k), zi + k, has_dn, rup_send, up_dev),
            (zi - k, below(k), zn if k == 1 else zi - k, has_up, rdn_send, dn_dev),
        ):
            @pl.when(there())
            def _(j=j, behind=behind):
                fold(j, i, k)

                @pl.when(behind)
                def _():
                    z_wait(t.layer, j, i)
                    combine(col(j, i), [z_in.at[t.layer, j, i]])

            t.go(col(j, i), z_in.at[t.layer, slot, i], lambda layer, sends=sends: sends.at[layer, k, i],
                 z_recv.at[t.layer, slot, i], dev, there)

    def z_wait(layer, slot, i):
        ref = z_in.at[layer, slot, i]
        remote(ref, ref, rup_send.at[0, 0, 0], z_recv.at[layer, slot, i], up_dev).wait_recv()

    def home(layer, col, i, fold):
        fold(zi, i, 0)
        total[...] = state[i].astype(jnp.float32) + col(zi, i)[...].astype(jnp.float32)
        for cond, slot in ((has_dn, zi), (has_up, zn)):
            @pl.when(cond)
            def _(slot=slot):
                z_wait(layer, slot, i)
                total[...] = total[...] + z_in[layer, slot, i].astype(jnp.float32)

        state[i] = total[...].astype(jnp.bfloat16)

    def hidden_sum(layer, g):
        wait_weight(0, g)
        flat = acts[layer, g].reshape(group_rows, half)
        pre[g] = lax.dot_general(
            flat, up_v[g].reshape(CORES * BLOCK, half), (((1,), (1,)), ((), ())), preferred_element_type=jnp.float32)
        swap_pre(g).start()

    def swap_pre(g):
        return remote(pre.at[g], pre_in.at[g], pre_sem.at[0, g], pre_sem.at[1, g], p_dev)

    def spread(g):
        wait_weight(1, g)
        swap_pre(g).wait_recv()
        both = pre[g] + pre_in[g]
        active = (jnp.maximum(both, 0.0) * live_ref[pl.ds(g, 1), :]).astype(jnp.bfloat16)
        for at in range(0, half, CHUNK):
            cols = pl.ds(at, min(CHUNK, half - at))
            made = jnp.dot(active, down_v[g, :, :, cols].reshape(CORES * BLOCK, -1), preferred_element_type=jnp.float32)
            part[g, :, :, :, cols] = made.astype(jnp.bfloat16).reshape(zn, CORES, rows, -1)

    def plane(layer):
        t = Sender(layer)
        for i in parts:
            t.x(me_o, zi, i, 0)
            t.up(me_o, zi, i, 0, lambda: has_up)
            t.dn(me_o, zi, i, 0, lambda: has_dn)

        def onward(i):
            return lambda j, there, slot: t.x(me_o, j, i, slot, there)

        def diagonal(j, slot):
            for i in parts:
                arrive(layer, diag, j, i)
                t.up(diag, j, i, slot, lambda: inner_lower)
                t.dn(diag, j, i, slot, lambda: inner_upper)

        for i in parts:
            arrive(layer, peer_y, zi, i)
            t.x(peer_y, zi, i, 2 * zn - 1)
            column(t, 1, i, onward(i))
        diagonal(zi, zn - 1)
        for i in parts:
            column(t, 2, i, onward(i))
        diagonal(twin, zn)
        for k in range(3, zn):
            for i in parts:
                column(t, k, i, onward(i))
        hidden_sum(layer, me_o)
        far = [low * (zn // 2 + n) + (1 - low) * (zn // 2 - 1 - n) for n in range(zn // 2)]
        for n, j in enumerate(far):
            for i in parts:
                arrive(layer, diag, j, i)
                t.dn(diag, j, i, zn - 1 + n, lambda: inner_lower)
                t.up(diag, j, i, zn - 1 + n, lambda: inner_upper)
        spread(me_o)
        for j in range(zn):
            for i in parts:
                arrive(layer, peer_x, j, i)
        hidden_sum(layer, peer_x)
        for k in range(1, zn):
            for j, there in ((zi - k, zi - k >= 0), (zi + k, zi + k < zn)):
                for i in parts:
                    when(there, lambda j=j, i=i: arrive(layer, peer_y, j, i))
        hidden_sum(layer, peer_y)
        hidden_sum(layer, diag)
        spread(peer_x)

        def away(k):
            return ((zi + k, above(k), k), (zi - k, below(k), zn - 1 + k))

        def give_x(g, j, i, slot, to, cond=always):
            t.go(part.at[g, j, i], x_in.at[to, i], lambda layer: rx_send.at[slot, i], x_recv.at[to, i], x_dev, cond)

        def give_y(g, j, i, slot, to, cond=always):
            t.go(part.at[g, j, i], y_in.at[to, i], lambda layer: ry_send.at[slot, i], y_recv.at[to, i], y_dev, cond)

        for k in range(zn - 1, 0, -1):
            for j, there, slot in away(k):
                for i in parts:
                    give_x(peer_x, j, i, slot, j, there)
        spread(peer_y)
        for k in range(zn - 1, 0, -1):
            for j, there, slot in away(k):
                for i in parts:
                    give_y(peer_y, j, i, slot, j, there)
        spread(diag)

        def relay_wait(j, i):
            ref = r_in.at[j, i]
            remote(ref, ref, rup_send.at[0, 0, 0], r_recv.at[j, i], up_dev).wait_recv()

        def relayed(j, i, cond):
            @pl.when(cond)
            def _():
                relay_wait(j, i)
                combine(part.at[diag, j, i], [r_in.at[j, i]])

        for n, j in enumerate(reversed(far)):
            for i in parts:
                relayed(j, i, inner)
                for sends, dev, cond in ((rup_send, up_dev, lower), (rdn_send, dn_dev, upper)):
                    t.go(part.at[diag, j, i], r_in.at[j, i],
                         lambda layer, n=n, i=i, sends=sends: sends.at[layer, zn + n, i],
                         r_recv.at[j, i], dev, lambda cond=cond: cond)

        def col(j, i):
            return part.at[me_o, j, i]

        def x_wait(slot, i):
            ref = x_in.at[slot, i]
            remote(ref, ref, rx_send.at[0, 0], x_recv.at[slot, i], x_dev).wait_recv()

        def fold(j, i, k):
            x_wait(j, i)
            combine(col(j, i), [x_in.at[j, i]])

        for k in range(zn - 1, 2, -1):
            for i in parts:
                line(t, col, k, i, fold)
        for i in parts:
            relayed(twin, i, inner)
            give_y(diag, twin, i, 2 * zn - 1, zn)
        for i in parts:
            line(t, col, 2, i, fold)
        for i in parts:
            relayed(zi, i, inner)
            give_x(diag, zi, i, 2 * zn - 1, zn)
        for i in parts:
            give_x(peer_x, zi, i, 0, zi)
        for i in parts:
            line(t, col, 1, i, fold)
        for i in parts:
            x_wait(zn, i)
            combine(part.at[peer_y, zi, i], [x_in.at[zn, i]])
            give_y(peer_y, zi, i, 0, zi)
        for i in parts:
            home(layer, col, i, fold)
        return t.log

    def beside(layer):
        t = Sender(layer)
        for i in parts:
            t.y(me_o, zi, i, 0)
            t.up(me_o, zi, i, 0, lambda: has_up)
            t.dn(me_o, zi, i, 0, lambda: has_dn)

        def onward(i, k):
            def run(j, there, slot):
                if k == 1:
                    sign = -1 if slot == k else 1
                    t.x(me_o, j, i, slot, lambda: zi + sign == twin)
                t.y(me_o, j, i, slot, there)
            return run

        for k in range(1, zn):
            for i in parts:
                column(t, k, i, onward(i, k))
            if k == 1:
                for i in parts:
                    arrive(layer, peer_x, twin, i)
                    t.y(peer_x, twin, i, 2 * zn - 1)

        def col(j, i):
            return y_in.at[j, i]

        def y_wait(slot, i):
            ref = y_in.at[slot, i]
            remote(ref, ref, ry_send.at[0, 0], y_recv.at[slot, i], y_dev).wait_recv()

        def fold(j, i, k):
            y_wait(j, i)
            if k == 1:
                @pl.when(j == twin)
                def _():
                    remote(q_in.at[i], q_in.at[i], rx_send.at[2 * zn, i], q_recv.at[i], x_dev).wait_recv()
                    combine(col(j, i), [q_in.at[i]])

        for k in range(zn - 1, 1, -1):
            for i in parts:
                line(t, col, k, i, fold)
        for i in parts:
            y_wait(zn, i)
            t.go(y_in.at[zn, i], q_in.at[i], lambda layer, i=i: rx_send.at[2 * zn, i], q_recv.at[i], x_dev)
        for i in parts:
            line(t, col, 1, i, fold)
        for i in parts:
            home(layer, col, i, fold)
        return t.log

    logs = {}

    def sublayer(layer, carry):
        values = state[...].astype(jnp.float32)
        mean = jnp.sum(values, axis=2, keepdims=True) / half
        centered = values - mean
        spread_of = jnp.sum(centered * centered, axis=2, keepdims=True)
        stat[layer, 0] = jnp.broadcast_to(mean, (CORES, rows, BLOCK))
        stat[layer, 1] = jnp.broadcast_to(spread_of, (CORES, rows, BLOCK))
        swap_stat = remote(stat.at[layer], stat_in.at[layer], ssem.at[0, layer], ssem.at[1, layer], p_dev)
        swap_stat.start()
        swap_stat.wait()
        other_mean = stat_in[layer, 0][:, :, :1]
        other_spread = stat_in[layer, 1][:, :, :1]
        full_mean = (mean + other_mean) * 0.5
        apart = mean - other_mean
        var = (spread_of + other_spread + apart * apart * (half / 2)) / width
        gain = gains_ref[pl.ds(layer, 1), mine]
        acts[layer, me_o, zi] = (
            (values - full_mean) * lax.rsqrt(var + 1e-05) * gain.reshape(1, 1, half)).astype(jnp.bfloat16)

        @pl.when(hi == layer)
        def _():
            logs["plane"] = plane(layer)

        @pl.when(hi != layer)
        def _():
            logs["beside"] = beside(layer)

        return carry

    lax.fori_loop(0, LAYERS, sublayer, 0)

    last = remote(state.at[1 - core], out_in, osem.at[0], osem.at[1], p_dev)
    last.start()
    out_ref[:, mine] = state[core]
    for name, layer in (("plane", hi), ("beside", 1 - hi)):
        for send, cond in logs[name]:
            when(cond(), lambda send=send, layer=layer: remote(
                out_in, out_in, send(layer), osem.at[1], x_dev).wait_send())
    for n in range(len(blocks)):
        for g in range(owners):
            give(n, g).wait_send()
    for g in range(owners):
        swap_pre(g).wait_send()
    last.wait()
    out_ref[:, theirs] = out_in[...]


def scratch_plan(owners, batches, rows, width):
    zn = batches // CORES
    half = width // CORES
    bf, full = jnp.bfloat16, jnp.float32
    shard = (CORES, rows, half)
    return [
        (shard, bf),
        ((LAYERS, owners, zn) + shard, bf),
        ((owners, CORES, BLOCK, half), bf),
        ((owners, CORES, BLOCK, half), bf),
        ((owners, batches * rows, CORES * BLOCK), full),
        ((owners, batches * rows, CORES * BLOCK), full),
        ((owners, zn) + shard, bf),
        ((zn + 1,) + shard, bf),
        ((zn + 1,) + shard, bf),
        (shard, bf),
        ((LAYERS, zn + 1) + shard, bf),
        ((zn,) + shard, bf),
        ((LAYERS, 2, CORES, rows, BLOCK), full),
        ((LAYERS, 2, CORES, rows, BLOCK), full),
        ((rows, half), bf),
        ((rows, half), full),
    ]


def scratch_bytes(plan):
    total = 0
    for shape, kind in plan:
        size = jnp.dtype(kind).itemsize
        for extent in shape:
            size *= extent
        total += size
    return total


def run_sublayers(owners, batches, hidden, gains, live, up_send, down_send):
    rows, width = hidden.shape
    zn = batches // CORES
    plan = scratch_plan(owners, batches, rows, width)
    dma = pltpu.SemaphoreType.DMA
    sems = [
        (2, 3, owners), (2,), (2,), (2, LAYERS), (2, owners), (LAYERS, owners, zn, CORES),
        (LAYERS, 2 * zn, CORES), (LAYERS, 2 * zn, CORES), (LAYERS, 2 * zn, CORES), (LAYERS, 2 * zn, CORES),
        (2 * zn + 1, CORES), (2 * zn, CORES), (LAYERS, 2 * zn, CORES), (LAYERS, 2 * zn, CORES),
        (zn + 1, CORES), (zn + 1, CORES), (CORES,), (LAYERS, zn + 1, CORES), (zn, CORES),
    ]
    vmem = pl.BlockSpec(memory_space=pltpu.VMEM)
    hbm = pl.BlockSpec(memory_space=pl.ANY)
    return pl.pallas_call(
        functools.partial(sublayers_kernel, owners, batches),
        out_shape=jax.ShapeDtypeStruct((rows, width), jnp.bfloat16),
        in_specs=[vmem, vmem, vmem, hbm, hbm],
        out_specs=vmem,
        scratch_shapes=[pltpu.VMEM(s, d) for s, d in plan] + [dma(s) for s in sems],
        compiler_params=pltpu.CompilerParams(
            collective_id=0, has_side_effects=True, vmem_limit_bytes=VMEM_BUDGET),
        name="sublayers",
    )(hidden, gains, live, up_send, down_send)


def fetch_kernel(owners, batches, held, pick_ref, up_ref, down_ref, live_ref, up_out, down_out, buf, isem, osem):
    sender = lax.axis_index("owner") * batches + lax.axis_index("batch")

    def read(i):
        g = i % owners
        at = jnp.minimum(pick_ref[g, sender], held - 1)
        src = up_ref if i < owners else down_ref
        return pltpu.make_async_copy(src.at[at], buf.at[i], isem.at[i])

    def write(i):
        dst = up_out if i < owners else down_out
        return pltpu.make_async_copy(buf.at[i], dst.at[i % owners], osem.at[i])

    for i in range(2 * owners):
        read(i).start()
    first = sender - sender % CORES
    for g in range(owners):
        for n in range(CORES):
            live = (pick_ref[g, first + n] < held).astype(jnp.float32)
            live_ref[g:g + 1, n * BLOCK:(n + 1) * BLOCK] = jnp.full((1, BLOCK), live, jnp.float32)
    for i in range(2 * owners):
        read(i).wait()
        write(i).start()
    for i in range(2 * owners):
        write(i).wait()


def fetch(owners, batches, up_rows, down_rows, pick):
    width = up_rows.shape[1]
    held = up_rows.shape[0] // BLOCK
    hbm = pl.BlockSpec(memory_space=pl.ANY)
    sent = jax.ShapeDtypeStruct((owners, BLOCK, width), up_rows.dtype)
    return pl.pallas_call(
        functools.partial(fetch_kernel, owners, batches, held),
        out_shape=(jax.ShapeDtypeStruct((owners, CORES * BLOCK), jnp.float32), sent, sent),
        in_specs=[pl.BlockSpec(memory_space=pltpu.SMEM), hbm, hbm],
        out_specs=(pl.BlockSpec(memory_space=pltpu.VMEM), hbm, hbm),
        scratch_shapes=[
            pltpu.VMEM((2 * owners, BLOCK, width), up_rows.dtype),
            pltpu.SemaphoreType.DMA((2 * owners,)),
            pltpu.SemaphoreType.DMA((2 * owners,)),
        ],
        compiler_params=pltpu.CompilerParams(vmem_limit_bytes=VMEM_BUDGET),
        name="fetch",
    )(pick, up_rows.reshape(held, BLOCK, width), down_rows.reshape(held, BLOCK, width))


def stay_body(hidden, gains, up_rows, down_rows, pick):
    owners = lax.axis_size("owner")
    batches = lax.axis_size("batch")
    live, up_send, down_send = fetch(owners, batches, up_rows, down_rows, pick)
    return run_sublayers(owners, batches, hidden, gains, live, up_send, down_send)


def normalize(rows_in, gain_row):
    values = rows_in.astype(jnp.float32)
    row_mean = jnp.mean(values, axis=1, keepdims=True)
    centered = values - row_mean
    row_var = jnp.mean(centered * centered, axis=1, keepdims=True)
    return (centered * lax.rsqrt(row_var + 1e-05) * gain_row[None, :]).astype(jnp.bfloat16)


def body(hidden, gains, up_rows, down_rows, pick):
    owners = lax.axis_size("owner")
    batches = lax.axis_size("batch")
    group_at = lax.axis_index("owner")
    lane_at = lax.axis_index("batch")
    held_blocks = up_rows.shape[0] // BLOCK
    model_width = up_rows.shape[1]
    local_rows = hidden.shape[0]
    _, up_send, down_send = fetch(owners, batches, up_rows, down_rows, pick)
    group_picks = lax.dynamic_slice_in_dim(pick, group_at, 1, 0)[0]
    live_slots = (group_picks[jnp.arange(owners) * batches + lane_at] < held_blocks).astype(
        jnp.float32
    )
    up_recv, down_recv = (
        lax.all_to_all(up_send, "owner", split_axis=0, concat_axis=0, tiled=True),
        lax.all_to_all(down_send, "owner", split_axis=0, concat_axis=0, tiled=True),
    )
    per_layer = owners // LAYERS
    residual = hidden
    for layer_at in range(LAYERS):
        first_slot = layer_at * per_layer
        up_part = up_recv[first_slot : first_slot + per_layer]
        down_part = down_recv[first_slot : first_slot + per_layer]
        keep_slots = live_slots[first_slot : first_slot + per_layer]
        up_flat = up_part.reshape(per_layer * BLOCK, model_width)
        down_flat = down_part.reshape(per_layer * BLOCK, model_width)
        neuron_mask = jnp.repeat(keep_slots, BLOCK)
        normed = normalize(residual, gains[layer_at])

        def expand(
            rows_piece,
            row_start,
            up_part=up_part,
            up_flat=up_flat,
            keep_slots=keep_slots,
            neuron_mask=neuron_mask,
        ):
            pre_act = lax.dot_general(
                rows_piece, up_flat, (((1,), (1,)), ((), ())), preferred_element_type=jnp.float32
            )
            return (jnp.maximum(pre_act, 0.0) * neuron_mask[None, :]).astype(jnp.bfloat16)

        active = expand(lax.all_gather(normed, "batch", axis=0, tiled=True), jnp.int32(0))

        def contract(
            row_start,
            row_count,
            active=active,
            down_part=down_part,
            down_flat=down_flat,
            keep_slots=keep_slots,
        ):
            return jnp.dot(active, down_flat, preferred_element_type=jnp.float32)

        summed = lax.psum_scatter(
            contract(jnp.int32(0), lax.axis_size("batch") * local_rows).astype(jnp.bfloat16),
            "batch",
            scatter_dimension=0,
            tiled=True,
        ).astype(jnp.float32)
        residual = (residual.astype(jnp.float32) + summed).astype(jnp.bfloat16)
    return residual


def solution(mesh):
    in_specs = (
        P(("owner", "batch"), None),
        P(),
        P(("owner", "batch"), None),
        P(("owner", "batch"), None),
        P(),
    )
    out_specs = P(("owner", "batch"), None)
    owners, batches = mesh.shape["owner"], mesh.shape["batch"]

    def whole(hidden, gains, up_rows, down_rows, pick):
        rows = hidden.shape[0] // (owners * batches)
        plan = scratch_plan(owners, batches, rows, hidden.shape[1])
        line = batches == 2 * TWINS * CORES
        fits = line and owners == 2 * LAYERS and scratch_bytes(plan) * 5 < VMEM_BUDGET * 4
        chosen = stay_body if fits else body
        return jax.shard_map(chosen, mesh=mesh, in_specs=in_specs, out_specs=out_specs, check_vma=False)(
            hidden, gains, up_rows, down_rows, pick)

    return whole
```

```python
import functools

import jax
import jax.numpy as jnp
from jax import lax
from jax.experimental import pallas as pl
from jax.experimental.pallas import tpu as pltpu
from jax.sharding import PartitionSpec as P

BLOCK = 128
LAYERS = 2
CORES = 2
TWINS = 2
VMEM_BUDGET = 40 * 1024 * 1024
FETCH_BUDGET = 40 * 1024 * 1024
CHUNK = 1024


def sublayers_kernel(
    owners, batches,
    hidden_ref, gains_ref, live_ref, up_hbm, down_hbm, out_ref,
    state, acts, up_v, down_v, pre, pre_in, part, x_in, y_in, q_in, z_in, r_in, stat, stat_in, out_in, total, normed,
    wsem, hsem, osem, ssem, pre_sem, ag_recv, x_send, y_send, up_send, dn_send,
    rx_send, ry_send, rup_send, rdn_send, x_recv, y_recv, q_recv, z_recv, r_recv,
):
    zn = batches // CORES
    per_layer = owners // LAYERS
    rows, width = hidden_ref.shape
    half = width // CORES
    group_rows = batches * rows
    me_o = lax.axis_index("owner")
    me_b = lax.axis_index("batch")
    hi, lo = me_o // per_layer, me_o % per_layer
    zi, core = me_b // CORES, me_b % CORES
    other = 1 - core
    peer_x = hi * per_layer + (1 - lo)
    peer_y = (1 - hi) * per_layer + lo
    diag = (1 - hi) * per_layer + (1 - lo)
    x_dev, y_dev = (peer_x, me_b), (peer_y, me_b)
    p_dev = (me_o, zi * CORES + 1 - core)
    up_dev, dn_dev = (me_o, me_b + CORES), (me_o, me_b - CORES)
    has_up, has_dn = zi < zn - 1, zi > 0
    lower = zi < zn // 2
    upper = zi >= zn // 2
    low = lower.astype(jnp.int32)
    twin = zi + 1 - 2 * (zi % 2)
    inner = jnp.logical_and(zi > 0, zi < zn - 1)
    outer = jnp.logical_not(inner)
    inner_lower, inner_upper = jnp.logical_and(inner, lower), jnp.logical_and(inner, upper)
    mine = pl.ds(pl.multiple_of(core * half, 128), half)
    theirs = pl.ds(pl.multiple_of((1 - core) * half, 128), half)
    parts = range(CORES)

    def remote(src, dst, send, recv, dev):
        return pltpu.make_async_remote_copy(
            src_ref=src, dst_ref=dst, send_sem=send, recv_sem=recv,
            device_id=dev, device_id_type=pl.DeviceIdType.MESH)

    def always():
        return True

    def when(cond, run):
        if cond is True:
            run()
        else:
            pl.when(cond)(run)

    barrier = pltpu.get_barrier_semaphore()
    for cond, dev in ((True, x_dev), (True, y_dev), (True, p_dev), (has_up, up_dev), (has_dn, dn_dev)):
        when(cond, lambda dev=dev: pl.semaphore_signal(
            barrier, inc=1, device_id=dev, device_id_type=pl.DeviceIdType.MESH))
    normed[...] = normalize(hidden_ref[...], gains_ref[0])
    acts[0, me_o, zi, core] = normed[:, mine]
    state[core] = hidden_ref[:, mine]
    pl.semaphore_wait(barrier, 3 + has_up.astype(jnp.int32) + has_dn.astype(jnp.int32))

    swap_normed = remote(normed.at[:, theirs], acts.at[0, me_o, zi, core], hsem.at[0], hsem.at[1], p_dev)
    swap_state = remote(hidden_ref.at[:, theirs], state.at[core], hsem.at[2], hsem.at[3], p_dev)
    swap_normed.start()
    swap_state.start()

    blocks = ((up_hbm, up_v), (down_hbm, down_v))

    def keep(n, g):
        hbm, vmem = blocks[n]
        return pltpu.make_async_copy(hbm.at[g, :, mine], vmem.at[g, core], wsem.at[n, 0, g])

    def give(n, g):
        hbm, vmem = blocks[n]
        return remote(hbm.at[g, :, theirs], vmem.at[g, core], wsem.at[n, 1, g], wsem.at[n, 2, g], p_dev)

    def wait_weight(n, g):
        keep(n, g).wait()
        give(n, g).wait_recv()

    class Sender:
        def __init__(self, layer):
            self.layer, self.log = layer, []

        def go(self, src, dst, send, recv, dev, cond=always):
            when(cond(), lambda: remote(src, dst, send(self.layer), recv, dev).start())
            self.log.append((send, cond))

        def spread_piece(self, sems, g, j, i, slot, dev, cond):
            ref = acts.at[self.layer, g, j, i]
            self.go(ref, ref, lambda layer: sems.at[layer, slot, i], ag_recv.at[self.layer, g, j, i], dev, cond)

        def x(self, g, j, i, slot, cond=always):
            self.spread_piece(x_send, g, j, i, slot, x_dev, cond)

        def y(self, g, j, i, slot, cond=always):
            self.spread_piece(y_send, g, j, i, slot, y_dev, cond)

        def up(self, g, j, i, slot, cond):
            self.spread_piece(up_send, g, j, i, slot, up_dev, cond)

        def dn(self, g, j, i, slot, cond):
            self.spread_piece(dn_send, g, j, i, slot, dn_dev, cond)

    def arrive(layer, g, j, i):
        ref = acts.at[layer, g, j, i]
        remote(ref, ref, x_send.at[0, 0, 0], ag_recv.at[layer, g, j, i], x_dev).wait_recv()

    def below(k):
        return lambda: zi - k >= 0

    def above(k):
        return lambda: zi + k < zn

    def column(t, k, i):
        for j, there, send, more in ((zi - k, below(k), t.up, has_up), (zi + k, above(k), t.dn, has_dn)):
            when(there(), lambda j=j: arrive(t.layer, me_o, j, i))
            if k < zn - 1:
                send(me_o, j, i, k, lambda there=there, more=more: jnp.logical_and(there(), more))

    def across(send, k, i):
        send(me_o, zi - k, i, k, below(k))
        send(me_o, zi + k, i, zn - 1 + k, above(k))

    def combine(dst, terms):
        total = dst[...].astype(jnp.float32)
        for term in terms:
            total = total + term[...].astype(jnp.float32)
        dst[...] = total.astype(jnp.bfloat16)

    def line(t, col, k, i, fold):
        for j, there, slot, behind, sends, dev in (
            (zi + k, above(k), zi + k, has_dn, rup_send, up_dev),
            (zi - k, below(k), zn if k == 1 else zi - k, has_up, rdn_send, dn_dev),
        ):
            @pl.when(there())
            def _(j=j, behind=behind):
                fold(j, i, k)

                @pl.when(behind)
                def _():
                    z_wait(t.layer, j, i)
                    combine(col(j, i), [z_in.at[t.layer, j, i]])

            t.go(col(j, i), z_in.at[t.layer, slot, i], lambda layer, sends=sends: sends.at[layer, k, i],
                 z_recv.at[t.layer, slot, i], dev, there)

    def z_wait(layer, slot, i):
        ref = z_in.at[layer, slot, i]
        remote(ref, ref, rup_send.at[0, 0, 0], z_recv.at[layer, slot, i], up_dev).wait_recv()

    def home(layer, col, i, fold):
        fold(zi, i, 0)
        total[...] = state[i].astype(jnp.float32) + col(zi, i)[...].astype(jnp.float32)
        for cond, slot in ((has_dn, zi), (has_up, zn)):
            @pl.when(cond)
            def _(slot=slot):
                z_wait(layer, slot, i)
                total[...] = total[...] + z_in[layer, slot, i].astype(jnp.float32)

        state[i] = total[...].astype(jnp.bfloat16)

    def hidden_sum(layer, g):
        wait_weight(0, g)
        flat = acts[layer, g].reshape(group_rows, half)
        pre[g] = lax.dot_general(
            flat, up_v[g].reshape(CORES * BLOCK, half), (((1,), (1,)), ((), ())), preferred_element_type=jnp.float32)
        swap_pre(g).start()

    def swap_pre(g):
        return remote(pre.at[g], pre_in.at[g], pre_sem.at[0, g], pre_sem.at[1, g], p_dev)

    def spread(g):
        wait_weight(1, g)
        swap_pre(g).wait_recv()
        both = pre[g] + pre_in[g]
        active = (jnp.maximum(both, 0.0) * live_ref[pl.ds(g, 1), :]).astype(jnp.bfloat16)
        for at in range(0, half, CHUNK):
            cols = pl.ds(at, min(CHUNK, half - at))
            made = jnp.dot(active, down_v[g, :, :, cols].reshape(CORES * BLOCK, -1), preferred_element_type=jnp.float32)
            part[g, :, :, :, cols] = made.astype(jnp.bfloat16).reshape(zn, CORES, rows, -1)

    def opening(t, toward):
        for n, i in enumerate((core, other)):
            if n:
                @pl.when(t.layer == 0)
                def _():
                    swap_normed.wait_recv()

            toward(me_o, zi, i, 0)
            t.up(me_o, zi, i, 0, lambda: has_up)
            t.dn(me_o, zi, i, 0, lambda: has_dn)

        @pl.when(t.layer == 0)
        def _():
            for n in range(len(blocks)):
                for g in range(owners):
                    keep(n, g).start()
                    give(n, g).start()
            swap_state.wait_recv()

    def plane(layer):
        t = Sender(layer)
        opening(t, t.x)
        far = [low * (zn // 2 + n) + (1 - low) * (zn // 2 - 1 - n) for n in range(zn // 2)]

        def diagonal(j, i, slot):
            arrive(layer, diag, j, i)
            t.up(diag, j, i, slot, lambda: inner_lower)
            t.dn(diag, j, i, slot, lambda: inner_upper)

        def relay(n, i):
            arrive(layer, diag, far[n], i)
            t.dn(diag, far[n], i, zn - 1 + n, lambda: inner_lower)
            t.up(diag, far[n], i, zn - 1 + n, lambda: inner_upper)

        for i in parts:
            arrive(layer, peer_y, zi, i)
            t.x(peer_y, zi, i, 2 * zn - 1)
            column(t, 1, i)
        for i in parts:
            across(t.x, 1, i)
        for i in parts:
            diagonal(zi, i, zn - 1)
            column(t, 2, i)
            across(t.x, 2, i)
        for i in parts:
            diagonal(twin, i, zn)
            for k in range(3, zn):
                column(t, k, i)
                across(t.x, k, i)
            relay(0, i)
        hidden_sum(layer, me_o)
        for n in range(1, zn // 2):
            for i in parts:
                relay(n, i)
        spread(me_o)
        for j in range(zn):
            for i in parts:
                arrive(layer, peer_x, j, i)
        hidden_sum(layer, peer_x)
        for k in range(1, zn):
            for j, there in ((zi - k, below(k)), (zi + k, above(k))):
                for i in parts:
                    when(there(), lambda j=j, i=i: arrive(layer, peer_y, j, i))
        hidden_sum(layer, peer_y)
        hidden_sum(layer, diag)

        def away(k):
            return ((zi + k, above(k), k), (zi - k, below(k), zn - 1 + k))

        def give_x(g, j, i, slot, to, cond=always):
            t.go(part.at[g, j, i], x_in.at[to, i], lambda layer: rx_send.at[slot, i], x_recv.at[to, i], x_dev, cond)

        def give_y(g, j, i, slot, to, cond=always):
            t.go(part.at[g, j, i], y_in.at[to, i], lambda layer: ry_send.at[slot, i], y_recv.at[to, i], y_dev, cond)

        def relay_wait(j, i):
            ref = r_in.at[j, i]
            remote(ref, ref, rup_send.at[0, 0, 0], r_recv.at[j, i], up_dev).wait_recv()

        def relayed(j, i):
            @pl.when(inner)
            def _():
                relay_wait(j, i)
                combine(part.at[diag, j, i], [r_in.at[j, i]])

        def give_z(n, i, place):
            for sends, dev, side in ((rup_send, up_dev, lower), (rdn_send, dn_dev, upper)):
                t.go(part.at[diag, far[n], i], r_in.at[far[n], i],
                     lambda layer, sends=sends: sends.at[layer, zn + n, i],
                     r_recv.at[far[n], i], dev, lambda side=side: jnp.logical_and(side, place))

        def relay_in(n, i):
            relayed(far[n], i)
            give_z(n, i, inner)

        def col(j, i):
            return part.at[me_o, j, i]

        def x_wait(slot, i):
            ref = x_in.at[slot, i]
            remote(ref, ref, rx_send.at[0, 0], x_recv.at[slot, i], x_dev).wait_recv()

        def fold(j, i, k):
            x_wait(j, i)
            combine(col(j, i), [x_in.at[j, i]])

        spread(diag)
        for n in reversed(range(zn // 2)):
            for i in parts:
                give_z(n, i, outer)
        spread(peer_x)
        for k in range(zn - 1, 0, -1):
            for j, there, slot in away(k):
                for i in parts:
                    give_x(peer_x, j, i, slot, j, there)
        spread(peer_y)
        for k in range(zn - 1, 1, -1):
            for j, there, slot in away(k):
                for i in parts:
                    give_y(peer_y, j, i, slot, j, there)
        for i in parts:
            give_y(peer_y, 2 * zi - twin, i, 1, 2 * zi - twin, lambda: inner)
        for n in reversed(range(1, zn // 2)):
            for i in parts:
                relay_in(n, i)
        for i in parts:
            relay_in(0, i)
            for k in range(zn - 1, 2, -1):
                line(t, col, k, i, fold)
            relayed(twin, i)
            give_y(diag, twin, i, 2 * zn - 1, zn)
        for i in parts:
            give_y(peer_y, twin, i, zn, twin)
        for i in parts:
            relayed(zi, i)
            give_x(diag, zi, i, 2 * zn - 1, zn)
            line(t, col, 2, i, fold)
        for i in parts:
            give_x(peer_x, zi, i, 0, zi)
        for i in parts:
            line(t, col, 1, i, fold)
        for i in parts:
            x_wait(zn, i)
            combine(part.at[peer_y, zi, i], [x_in.at[zn, i]])
            give_y(peer_y, zi, i, 0, zi)
        for i in parts:
            home(layer, col, i, fold)
        return t.log

    def beside(layer):
        t = Sender(layer)
        opening(t, t.y)

        def beyond(send, i, near):
            for sign, slot in ((-1, 1), (1, zn)):
                send(me_o, zi + sign, i, slot, lambda sign=sign: (
                    zi + sign == twin if near else jnp.logical_and(inner, zi + sign != twin)))

        for i in parts:
            column(t, 1, i)
            beyond(t.x, i, True)
        for i in parts:
            beyond(t.y, i, True)
        for i in parts:
            arrive(layer, peer_x, twin, i)
            t.y(peer_x, twin, i, 2 * zn - 1)
            column(t, 2, i)
        for i in parts:
            beyond(t.y, i, False)
        for i in parts:
            across(t.y, 2, i)
        for k in range(3, zn):
            for i in parts:
                column(t, k, i)
                across(t.y, k, i)

        def col(j, i):
            return y_in.at[j, i]

        def y_wait(slot, i):
            ref = y_in.at[slot, i]
            remote(ref, ref, ry_send.at[0, 0], y_recv.at[slot, i], y_dev).wait_recv()

        def fold(j, i, k):
            y_wait(j, i)
            if k == 1:
                @pl.when(j == twin)
                def _():
                    remote(q_in.at[i], q_in.at[i], rx_send.at[2 * zn, i], q_recv.at[i], x_dev).wait_recv()
                    combine(col(j, i), [q_in.at[i]])

        for k in range(zn - 1, 1, -1):
            for i in parts:
                line(t, col, k, i, fold)
        for i in parts:
            y_wait(zn, i)
            t.go(y_in.at[zn, i], q_in.at[i], lambda layer, i=i: rx_send.at[2 * zn, i], q_recv.at[i], x_dev)
        for i in parts:
            line(t, col, 1, i, fold)
        for i in parts:
            home(layer, col, i, fold)
        return t.log

    logs = {}

    def renew(layer):
        values = state[...].astype(jnp.float32)
        mean = jnp.sum(values, axis=2, keepdims=True) / half
        centered = values - mean
        spread_of = jnp.sum(centered * centered, axis=2, keepdims=True)
        stat[layer, 0] = jnp.broadcast_to(mean, (CORES, rows, BLOCK))
        stat[layer, 1] = jnp.broadcast_to(spread_of, (CORES, rows, BLOCK))
        swap_stat = remote(stat.at[layer], stat_in.at[layer], ssem.at[0, layer], ssem.at[1, layer], p_dev)
        swap_stat.start()
        swap_stat.wait()
        other_mean = stat_in[layer, 0][:, :, :1]
        other_spread = stat_in[layer, 1][:, :, :1]
        full_mean = (mean + other_mean) * 0.5
        apart = mean - other_mean
        var = (spread_of + other_spread + apart * apart * (half / 2)) / width
        gain = gains_ref[pl.ds(layer, 1), mine]
        acts[layer, me_o, zi] = (
            (values - full_mean) * lax.rsqrt(var + 1e-05) * gain.reshape(1, 1, half)).astype(jnp.bfloat16)

    def sublayer(layer, carry):
        @pl.when(hi == layer)
        def _():
            logs["plane"] = plane(layer)

        @pl.when(hi != layer)
        def _():
            logs["beside"] = beside(layer)

        @pl.when(layer < LAYERS - 1)
        def _():
            renew(layer + 1)

        return carry

    lax.fori_loop(0, LAYERS, sublayer, 0)

    last = remote(state.at[1 - core], out_in, osem.at[0], osem.at[1], p_dev)
    last.start()
    out_ref[:, mine] = state[core]
    for name, layer in (("plane", hi), ("beside", 1 - hi)):
        for send, cond in logs[name]:
            when(cond(), lambda send=send, layer=layer: remote(
                out_in, out_in, send(layer), osem.at[1], x_dev).wait_send())
    for n in range(len(blocks)):
        for g in range(owners):
            give(n, g).wait_send()
    for g in range(owners):
        swap_pre(g).wait_send()
    swap_normed.wait_send()
    swap_state.wait_send()
    last.wait()
    out_ref[:, theirs] = out_in[...]


def scratch_plan(owners, batches, rows, width):
    zn = batches // CORES
    half = width // CORES
    bf, full = jnp.bfloat16, jnp.float32
    shard = (CORES, rows, half)
    return [
        (shard, bf),
        ((LAYERS, owners, zn) + shard, bf),
        ((owners, CORES, BLOCK, half), bf),
        ((owners, CORES, BLOCK, half), bf),
        ((owners, batches * rows, CORES * BLOCK), full),
        ((owners, batches * rows, CORES * BLOCK), full),
        ((owners, zn) + shard, bf),
        ((zn + 1,) + shard, bf),
        ((zn + 1,) + shard, bf),
        (shard, bf),
        ((LAYERS, zn + 1) + shard, bf),
        ((zn,) + shard, bf),
        ((LAYERS, 2, CORES, rows, BLOCK), full),
        ((LAYERS, 2, CORES, rows, BLOCK), full),
        ((rows, half), bf),
        ((rows, half), full),
        ((rows, width), bf),
    ]


def scratch_bytes(plan):
    total = 0
    for shape, kind in plan:
        size = jnp.dtype(kind).itemsize
        for extent in shape:
            size *= extent
        total += size
    return total


def run_sublayers(owners, batches, hidden, gains, live, up_send, down_send):
    rows, width = hidden.shape
    zn = batches // CORES
    plan = scratch_plan(owners, batches, rows, width)
    dma = pltpu.SemaphoreType.DMA
    sems = [
        (2, 3, owners), (4,), (2,), (2, LAYERS), (2, owners), (LAYERS, owners, zn, CORES),
        (LAYERS, 2 * zn, CORES), (LAYERS, 2 * zn, CORES), (LAYERS, 2 * zn, CORES), (LAYERS, 2 * zn, CORES),
        (2 * zn + 1, CORES), (2 * zn, CORES), (LAYERS, 2 * zn, CORES), (LAYERS, 2 * zn, CORES),
        (zn + 1, CORES), (zn + 1, CORES), (CORES,), (LAYERS, zn + 1, CORES), (zn, CORES),
    ]
    vmem = pl.BlockSpec(memory_space=pltpu.VMEM)
    hbm = pl.BlockSpec(memory_space=pl.ANY)
    return pl.pallas_call(
        functools.partial(sublayers_kernel, owners, batches),
        out_shape=jax.ShapeDtypeStruct((rows, width), jnp.bfloat16),
        in_specs=[vmem] * 5,
        out_specs=vmem,
        scratch_shapes=[pltpu.VMEM(s, d) for s, d in plan] + [dma(s) for s in sems],
        compiler_params=pltpu.CompilerParams(
            collective_id=0, has_side_effects=True, vmem_limit_bytes=VMEM_BUDGET),
        name="sublayers",
    )(hidden, gains, live, up_send, down_send)


def fetch_kernel(owners, batches, held, pick_ref, up_ref, down_ref, live_ref, up_out, down_out, sem):
    sender = lax.axis_index("owner") * batches + lax.axis_index("batch")

    def read(i):
        g = i % owners
        at = jnp.minimum(pick_ref[g, sender], held - 1)
        src, dst = (up_ref, up_out) if i < owners else (down_ref, down_out)
        return pltpu.make_async_copy(src.at[at], dst.at[g], sem.at[i])

    for i in range(2 * owners):
        read(i).start()
    first = sender - sender % CORES
    for g in range(owners):
        for n in range(CORES):
            live = (pick_ref[g, first + n] < held).astype(jnp.float32)
            live_ref[g:g + 1, n * BLOCK:(n + 1) * BLOCK] = jnp.full((1, BLOCK), live, jnp.float32)
    for i in range(2 * owners):
        read(i).wait()


def fetch(owners, batches, up_rows, down_rows, pick, near):
    width = up_rows.shape[1]
    held = up_rows.shape[0] // BLOCK
    hbm = pl.BlockSpec(memory_space=pl.ANY)
    vmem = pl.BlockSpec(memory_space=pltpu.VMEM)
    shape = (owners, BLOCK, width)
    sent = pltpu.VMEM(shape, up_rows.dtype) if near else jax.ShapeDtypeStruct(shape, up_rows.dtype)
    return pl.pallas_call(
        functools.partial(fetch_kernel, owners, batches, held),
        out_shape=(jax.ShapeDtypeStruct((owners, CORES * BLOCK), jnp.float32), sent, sent),
        in_specs=[pl.BlockSpec(memory_space=pltpu.SMEM), hbm, hbm],
        out_specs=(vmem, vmem, vmem) if near else (vmem, hbm, hbm),
        scratch_shapes=[pltpu.SemaphoreType.DMA((2 * owners,))],
        compiler_params=pltpu.CompilerParams(vmem_limit_bytes=FETCH_BUDGET),
        name="fetch",
    )(pick, up_rows.reshape(held, BLOCK, width), down_rows.reshape(held, BLOCK, width))


def stay_body(hidden, gains, up_rows, down_rows, pick):
    owners = lax.axis_size("owner")
    batches = lax.axis_size("batch")
    live, up_send, down_send = fetch(owners, batches, up_rows, down_rows, pick, True)
    return run_sublayers(owners, batches, hidden, gains, live, up_send, down_send)


def normalize(rows_in, gain_row):
    values = rows_in.astype(jnp.float32)
    row_mean = jnp.mean(values, axis=1, keepdims=True)
    centered = values - row_mean
    row_var = jnp.mean(centered * centered, axis=1, keepdims=True)
    return (centered * lax.rsqrt(row_var + 1e-05) * gain_row[None, :]).astype(jnp.bfloat16)


def body(hidden, gains, up_rows, down_rows, pick):
    owners = lax.axis_size("owner")
    batches = lax.axis_size("batch")
    group_at = lax.axis_index("owner")
    lane_at = lax.axis_index("batch")
    held_blocks = up_rows.shape[0] // BLOCK
    model_width = up_rows.shape[1]
    local_rows = hidden.shape[0]
    _, up_send, down_send = fetch(owners, batches, up_rows, down_rows, pick, False)
    group_picks = lax.dynamic_slice_in_dim(pick, group_at, 1, 0)[0]
    live_slots = (group_picks[jnp.arange(owners) * batches + lane_at] < held_blocks).astype(
        jnp.float32
    )
    up_recv, down_recv = (
        lax.all_to_all(up_send, "owner", split_axis=0, concat_axis=0, tiled=True),
        lax.all_to_all(down_send, "owner", split_axis=0, concat_axis=0, tiled=True),
    )
    per_layer = owners // LAYERS
    residual = hidden
    for layer_at in range(LAYERS):
        first_slot = layer_at * per_layer
        up_part = up_recv[first_slot : first_slot + per_layer]
        down_part = down_recv[first_slot : first_slot + per_layer]
        keep_slots = live_slots[first_slot : first_slot + per_layer]
        up_flat = up_part.reshape(per_layer * BLOCK, model_width)
        down_flat = down_part.reshape(per_layer * BLOCK, model_width)
        neuron_mask = jnp.repeat(keep_slots, BLOCK)
        normed = normalize(residual, gains[layer_at])

        def expand(
            rows_piece,
            row_start,
            up_part=up_part,
            up_flat=up_flat,
            keep_slots=keep_slots,
            neuron_mask=neuron_mask,
        ):
            pre_act = lax.dot_general(
                rows_piece, up_flat, (((1,), (1,)), ((), ())), preferred_element_type=jnp.float32
            )
            return (jnp.maximum(pre_act, 0.0) * neuron_mask[None, :]).astype(jnp.bfloat16)

        active = expand(lax.all_gather(normed, "batch", axis=0, tiled=True), jnp.int32(0))

        def contract(
            row_start,
            row_count,
            active=active,
            down_part=down_part,
            down_flat=down_flat,
            keep_slots=keep_slots,
        ):
            return jnp.dot(active, down_flat, preferred_element_type=jnp.float32)

        summed = lax.psum_scatter(
            contract(jnp.int32(0), lax.axis_size("batch") * local_rows).astype(jnp.bfloat16),
            "batch",
            scatter_dimension=0,
            tiled=True,
        ).astype(jnp.float32)
        residual = (residual.astype(jnp.float32) + summed).astype(jnp.bfloat16)
    return residual


def solution(mesh):
    in_specs = (
        P(("owner", "batch"), None),
        P(),
        P(("owner", "batch"), None),
        P(("owner", "batch"), None),
        P(),
    )
    out_specs = P(("owner", "batch"), None)
    owners, batches = mesh.shape["owner"], mesh.shape["batch"]

    def whole(hidden, gains, up_rows, down_rows, pick):
        rows = hidden.shape[0] // (owners * batches)
        plan = scratch_plan(owners, batches, rows, hidden.shape[1])
        line = batches == 2 * TWINS * CORES
        fits = line and owners == 2 * LAYERS and scratch_bytes(plan) * 5 < VMEM_BUDGET * 4
        chosen = stay_body if fits else body
        return jax.shard_map(chosen, mesh=mesh, in_specs=in_specs, out_specs=out_specs, check_vma=False)(
            hidden, gains, up_rows, down_rows, pick)

    return whole
```

```python
import functools

import jax
import jax.numpy as jnp
from jax import lax
from jax.experimental import pallas as pl
from jax.experimental.pallas import tpu as pltpu
from jax.sharding import PartitionSpec as P

BLOCK = 128
LAYERS = 2
CORES = 2
TWINS = 2
VMEM_BUDGET = 40 * 1024 * 1024
FETCH_BUDGET = 40 * 1024 * 1024
CHUNK = 1024


def sublayers_kernel(
    owners, batches,
    hidden_ref, gains_ref, live_ref, up_hbm, down_hbm, out_ref,
    state, acts, up_v, down_v, pre, pre_in, part, x_in, y_in, q_in, z_in, r_in, stat, stat_in, out_in, total, normed,
    wsem, hsem, osem, ssem, pre_sem, ag_recv, x_send, y_send, up_send, dn_send,
    rx_send, ry_send, rup_send, rdn_send, x_recv, y_recv, q_recv, z_recv, r_recv,
):
    zn = batches // CORES
    per_layer = owners // LAYERS
    rows, width = hidden_ref.shape
    half = width // CORES
    group_rows = batches * rows
    me_o = lax.axis_index("owner")
    me_b = lax.axis_index("batch")
    hi, lo = me_o // per_layer, me_o % per_layer
    zi, core = me_b // CORES, me_b % CORES
    other = 1 - core
    peer_x = hi * per_layer + (1 - lo)
    peer_y = (1 - hi) * per_layer + lo
    diag = (1 - hi) * per_layer + (1 - lo)
    x_dev, y_dev = (peer_x, me_b), (peer_y, me_b)
    p_dev = (me_o, zi * CORES + 1 - core)
    up_dev, dn_dev = (me_o, me_b + CORES), (me_o, me_b - CORES)
    has_up, has_dn = zi < zn - 1, zi > 0
    lower = zi < zn // 2
    upper = zi >= zn // 2
    low = lower.astype(jnp.int32)
    twin = zi + 1 - 2 * (zi % 2)
    inner = jnp.logical_and(zi > 0, zi < zn - 1)
    outer = jnp.logical_not(inner)
    inner_lower, inner_upper = jnp.logical_and(inner, lower), jnp.logical_and(inner, upper)
    mine = pl.ds(pl.multiple_of(core * half, 128), half)
    theirs = pl.ds(pl.multiple_of((1 - core) * half, 128), half)
    parts = range(CORES)

    def remote(src, dst, send, recv, dev):
        return pltpu.make_async_remote_copy(
            src_ref=src, dst_ref=dst, send_sem=send, recv_sem=recv,
            device_id=dev, device_id_type=pl.DeviceIdType.MESH)

    def always():
        return True

    def when(cond, run):
        if cond is True:
            run()
        else:
            pl.when(cond)(run)

    barrier = pltpu.get_barrier_semaphore()
    for cond, dev in ((True, x_dev), (True, y_dev), (True, p_dev), (has_up, up_dev), (has_dn, dn_dev)):
        when(cond, lambda dev=dev: pl.semaphore_signal(
            barrier, inc=1, device_id=dev, device_id_type=pl.DeviceIdType.MESH))
    normed[...] = normalize(hidden_ref[...], gains_ref[0])
    acts[0, me_o, zi, core] = normed[:, mine]
    state[core] = hidden_ref[:, mine]
    pl.semaphore_wait(barrier, 3 + has_up.astype(jnp.int32) + has_dn.astype(jnp.int32))

    swap_normed = remote(normed.at[:, theirs], acts.at[0, me_o, zi, core], hsem.at[0], hsem.at[1], p_dev)
    swap_state = remote(hidden_ref.at[:, theirs], state.at[core], hsem.at[2], hsem.at[3], p_dev)
    swap_normed.start()
    swap_state.start()

    blocks = ((up_hbm, up_v), (down_hbm, down_v))

    def keep(n, g):
        hbm, vmem = blocks[n]
        return pltpu.make_async_copy(hbm.at[g, :, mine], vmem.at[g, core], wsem.at[n, 0, g])

    def give(n, g):
        hbm, vmem = blocks[n]
        return remote(hbm.at[g, :, theirs], vmem.at[g, core], wsem.at[n, 1, g], wsem.at[n, 2, g], p_dev)

    def wait_weight(n, g):
        keep(n, g).wait()
        give(n, g).wait_recv()

    class Sender:
        def __init__(self, layer):
            self.layer, self.log, self.mute = layer, [], False

        def go(self, src, dst, send, recv, dev, cond=always):
            when(cond(), lambda: remote(src, dst, send(self.layer), recv, dev).start())
            if not self.mute:
                self.log.append((send, cond))

        def spread_piece(self, sems, g, j, i, slot, dev, cond):
            ref = acts.at[self.layer, g, j, i]
            self.go(ref, ref, lambda layer: sems.at[layer, slot, i], ag_recv.at[self.layer, g, j, i], dev, cond)

        def x(self, g, j, i, slot, cond=always):
            self.spread_piece(x_send, g, j, i, slot, x_dev, cond)

        def y(self, g, j, i, slot, cond=always):
            self.spread_piece(y_send, g, j, i, slot, y_dev, cond)

        def up(self, g, j, i, slot, cond):
            self.spread_piece(up_send, g, j, i, slot, up_dev, cond)

        def dn(self, g, j, i, slot, cond):
            self.spread_piece(dn_send, g, j, i, slot, dn_dev, cond)

    def arrive(layer, g, j, i):
        ref = acts.at[layer, g, j, i]
        remote(ref, ref, x_send.at[0, 0, 0], ag_recv.at[layer, g, j, i], x_dev).wait_recv()

    def below(k):
        return lambda: zi - k >= 0

    def above(k):
        return lambda: zi + k < zn

    def column(t, k, i):
        for j, there, send, more in ((zi - k, below(k), t.up, has_up), (zi + k, above(k), t.dn, has_dn)):
            when(there(), lambda j=j: arrive(t.layer, me_o, j, i))
            if k < zn - 1:
                send(me_o, j, i, k, lambda there=there, more=more: jnp.logical_and(there(), more))

    def across(send, k, i):
        send(me_o, zi - k, i, k, below(k))
        send(me_o, zi + k, i, zn - 1 + k, above(k))

    def combine(dst, terms):
        total = dst[...].astype(jnp.float32)
        for term in terms:
            total = total + term[...].astype(jnp.float32)
        dst[...] = total.astype(jnp.bfloat16)

    def line(t, col, k, i, fold):
        for j, there, slot, behind, sends, dev in (
            (zi + k, above(k), zi + k, has_dn, rup_send, up_dev),
            (zi - k, below(k), zn if k == 1 else zi - k, has_up, rdn_send, dn_dev),
        ):
            @pl.when(there())
            def _(j=j, behind=behind):
                fold(j, i, k)

                @pl.when(behind)
                def _():
                    z_wait(t.layer, j, i)
                    combine(col(j, i), [z_in.at[t.layer, j, i]])

            t.go(col(j, i), z_in.at[t.layer, slot, i], lambda layer, sends=sends: sends.at[layer, k, i],
                 z_recv.at[t.layer, slot, i], dev, there)

    def z_wait(layer, slot, i):
        ref = z_in.at[layer, slot, i]
        remote(ref, ref, rup_send.at[0, 0, 0], z_recv.at[layer, slot, i], up_dev).wait_recv()

    def home(layer, col, i, fold):
        fold(zi, i, 0)
        total[...] = state[i].astype(jnp.float32) + col(zi, i)[...].astype(jnp.float32)
        for cond, slot in ((has_dn, zi), (has_up, zn)):
            @pl.when(cond)
            def _(slot=slot):
                z_wait(layer, slot, i)
                total[...] = total[...] + z_in[layer, slot, i].astype(jnp.float32)

        state[i] = total[...].astype(jnp.bfloat16)

        @pl.when(layer < LAYERS - 1)
        def _():
            renew(layer + 1, i)

    def hidden_sum(layer, g):
        wait_weight(0, g)
        flat = acts[layer, g].reshape(group_rows, half)
        pre[g] = lax.dot_general(
            flat, up_v[g].reshape(CORES * BLOCK, half), (((1,), (1,)), ((), ())), preferred_element_type=jnp.float32)
        swap_pre(g).start()

    def swap_pre(g):
        return remote(pre.at[g], pre_in.at[g], pre_sem.at[0, g], pre_sem.at[1, g], p_dev)

    def spread(g):
        wait_weight(1, g)
        swap_pre(g).wait_recv()
        both = pre[g] + pre_in[g]
        active = (jnp.maximum(both, 0.0) * live_ref[pl.ds(g, 1), :]).astype(jnp.bfloat16)
        for at in range(0, half, CHUNK):
            cols = pl.ds(at, min(CHUNK, half - at))
            made = jnp.dot(active, down_v[g, :, :, cols].reshape(CORES * BLOCK, -1), preferred_element_type=jnp.float32)
            part[g, :, :, :, cols] = made.astype(jnp.bfloat16).reshape(zn, CORES, rows, -1)

    def opening(t, toward, sems):
        def out(i):
            toward(me_o, zi, i, 0)
            t.up(me_o, zi, i, 0, lambda: has_up)
            t.dn(me_o, zi, i, 0, lambda: has_dn)

        t.mute = True

        @pl.when(t.layer == 0)
        def _():
            out(core)
            swap_normed.wait_recv()
            out(other)
            for n in range(len(blocks)):
                for g in range(owners):
                    keep(n, g).start()
                    give(n, g).start()
            swap_state.wait_recv()

        @pl.when(t.layer > 0)
        def _():
            for i in parts:
                renew_done(t.layer, i)
                out(i)

        t.mute = False
        for i in parts:
            for used, cond in ((sems, always), (up_send, lambda: has_up), (dn_send, lambda: has_dn)):
                t.log.append((lambda layer, used=used, i=i: used.at[layer, 0, i], cond))

    def plane(layer):
        t = Sender(layer)
        opening(t, t.x, x_send)
        far = [low * (zn // 2 + n) + (1 - low) * (zn // 2 - 1 - n) for n in range(zn // 2)]

        def is_inner():
            return inner

        def is_outer():
            return outer

        def at_inner(g, j, i):
            when(inner, lambda: arrive(layer, g, j, i))

        def at_outer(g, j, i):
            when(outer, lambda: arrive(layer, g, j, i))

        def diagonal(j, i, slot):
            at_inner(diag, j, i)
            t.up(diag, j, i, slot, lambda: inner_lower)
            t.dn(diag, j, i, slot, lambda: inner_upper)

        def relay(n, i):
            at_inner(diag, far[n], i)
            t.dn(diag, far[n], i, zn - 1 + n, lambda: inner_lower)
            t.up(diag, far[n], i, zn - 1 + n, lambda: inner_upper)

        for i in parts:
            at_inner(peer_y, zi, i)
            t.x(peer_y, zi, i, 2 * zn - 1, is_inner)
            column(t, 1, i)
        for i in parts:
            across(t.x, 1, i)
        for i in parts:
            diagonal(zi, i, zn - 1)
            column(t, 2, i)
            across(t.x, 2, i)
        for i in parts:
            diagonal(twin, i, zn)
            for k in range(3, zn):
                column(t, k, i)
                across(t.x, k, i)
            relay(0, i)
        for i in parts:
            at_outer(peer_y, zi, i)
            t.x(peer_y, zi, i, 2 * zn - 1, is_outer)
        hidden_sum(layer, me_o)
        for n in range(1, zn // 2):
            for i in parts:
                relay(n, i)
        spread(me_o)

        def away(k):
            return ((zi + k, above(k), k), (zi - k, below(k), zn - 1 + k))

        def give_x(g, j, i, slot, to, cond=always):
            t.go(part.at[g, j, i], x_in.at[to, i], lambda layer: rx_send.at[slot, i], x_recv.at[to, i], x_dev, cond)

        def give_y(g, j, i, slot, to, cond=always):
            t.go(part.at[g, j, i], y_in.at[to, i], lambda layer: ry_send.at[slot, i], y_recv.at[to, i], y_dev, cond)

        def relay_wait(j, i):
            ref = r_in.at[j, i]
            remote(ref, ref, rup_send.at[0, 0, 0], r_recv.at[j, i], up_dev).wait_recv()

        def relayed(j, i):
            @pl.when(inner)
            def _():
                relay_wait(j, i)
                combine(part.at[diag, j, i], [r_in.at[j, i]])

        def give_z(n, i, place):
            for sends, dev, side in ((rup_send, up_dev, lower), (rdn_send, dn_dev, upper)):
                t.go(part.at[diag, far[n], i], r_in.at[far[n], i],
                     lambda layer, sends=sends: sends.at[layer, zn + n, i],
                     r_recv.at[far[n], i], dev, lambda side=side: jnp.logical_and(side, place))

        def relay_in(n, i):
            relayed(far[n], i)
            give_z(n, i, inner)

        def col(j, i):
            return part.at[me_o, j, i]

        def x_wait(slot, i):
            ref = x_in.at[slot, i]
            remote(ref, ref, rx_send.at[0, 0], x_recv.at[slot, i], x_dev).wait_recv()

        def fold(j, i, k):
            x_wait(j, i)
            combine(col(j, i), [x_in.at[j, i]])

        def wait_x():
            for j in range(zn):
                for i in parts:
                    arrive(layer, peer_x, j, i)

        def wait_y():
            for k in range(1, zn):
                for j, there in ((zi - k, below(k)), (zi + k, above(k))):
                    for i in parts:
                        when(there(), lambda j=j, i=i: arrive(layer, peer_y, j, i))

        def wait_diag():
            for j in [zi, twin] + far:
                for i in parts:
                    arrive(layer, diag, j, i)

        def send_x(place):
            for k in range(zn - 1, 0, -1):
                for j, there, slot in away(k):
                    for i in parts:
                        give_x(peer_x, j, i, slot, j, lambda there=there: jnp.logical_and(there(), place))

        def send_y(place):
            for k in range(zn - 1, 1, -1):
                for j, there, slot in away(k):
                    for i in parts:
                        give_y(peer_y, j, i, slot, j, lambda there=there: jnp.logical_and(there(), place))

        inside = inner.astype(jnp.int32)

        def either(at_in, at_out):
            return inside * at_in + (1 - inside) * at_out

        when(outer, wait_x)
        hidden_sum(layer, either(diag, peer_x))
        when(inner, wait_x)
        when(outer, wait_y)
        hidden_sum(layer, either(peer_x, peer_y))
        spread(either(diag, peer_x))
        send_x(outer)
        when(outer, lambda: spread(peer_y))
        send_y(outer)
        when(outer, wait_diag)
        when(inner, wait_y)
        hidden_sum(layer, either(peer_y, diag))
        when(inner, lambda: spread(peer_x))
        send_x(inner)
        spread(either(peer_y, diag))
        for n in reversed(range(zn // 2)):
            for i in parts:
                give_z(n, i, outer)
        send_y(inner)
        for i in parts:
            give_y(peer_y, 2 * zi - twin, i, 1, 2 * zi - twin, lambda: inner)
        for n in reversed(range(1, zn // 2)):
            for i in parts:
                relay_in(n, i)
        for i in parts:
            relay_in(0, i)
            for k in range(zn - 1, 2, -1):
                line(t, col, k, i, fold)
            relayed(twin, i)
            give_y(diag, twin, i, 2 * zn - 1, zn)
        for i in parts:
            give_y(peer_y, twin, i, zn, twin)
        for i in parts:
            relayed(zi, i)
            give_x(diag, zi, i, 2 * zn - 1, zn)
            line(t, col, 2, i, fold)
        for i in parts:
            give_x(peer_x, zi, i, 0, zi)
        for i in parts:
            line(t, col, 1, i, fold)
        for i in parts:
            x_wait(zn, i)
            combine(part.at[peer_y, zi, i], [x_in.at[zn, i]])
            give_y(peer_y, zi, i, 0, zi)
        for i in parts:
            home(layer, col, i, fold)
        return t.log

    def beside(layer):
        t = Sender(layer)
        opening(t, t.y, y_send)

        def beyond(send, i, near):
            for sign, slot in ((-1, 1), (1, zn)):
                send(me_o, zi + sign, i, slot, lambda sign=sign: (
                    zi + sign == twin if near else jnp.logical_and(inner, zi + sign != twin)))

        for i in parts:
            column(t, 1, i)
            beyond(t.x, i, True)
        for i in parts:
            beyond(t.y, i, True)
        for i in parts:
            when(inner, lambda i=i: arrive(layer, peer_x, twin, i))
            t.y(peer_x, twin, i, 2 * zn - 1, lambda: inner)
            column(t, 2, i)
        for i in parts:
            beyond(t.y, i, False)
        for i in parts:
            across(t.y, 2, i)
        for k in range(3, zn):
            for i in parts:
                column(t, k, i)
                across(t.y, k, i)
        for i in parts:
            when(outer, lambda i=i: arrive(layer, peer_x, twin, i))
            t.y(peer_x, twin, i, 2 * zn - 1, lambda: outer)

        def col(j, i):
            return y_in.at[j, i]

        def y_wait(slot, i):
            ref = y_in.at[slot, i]
            remote(ref, ref, ry_send.at[0, 0], y_recv.at[slot, i], y_dev).wait_recv()

        def fold(j, i, k):
            y_wait(j, i)
            if k == 1:
                @pl.when(j == twin)
                def _():
                    remote(q_in.at[i], q_in.at[i], rx_send.at[2 * zn, i], q_recv.at[i], x_dev).wait_recv()
                    combine(col(j, i), [q_in.at[i]])

        for k in range(zn - 1, 1, -1):
            for i in parts:
                line(t, col, k, i, fold)
        for i in parts:
            y_wait(zn, i)
            t.go(y_in.at[zn, i], q_in.at[i], lambda layer, i=i: rx_send.at[2 * zn, i], q_recv.at[i], x_dev)
        for i in parts:
            line(t, col, 1, i, fold)
        for i in parts:
            home(layer, col, i, fold)
        return t.log

    logs = {}

    def swap_stat(layer, i):
        return remote(stat.at[layer, i], stat_in.at[layer, i], ssem.at[0, layer, i], ssem.at[1, layer, i], p_dev)

    def renew(layer, i):
        values = state[i].astype(jnp.float32)
        mean = jnp.sum(values, axis=1, keepdims=True) / half
        centered = values - mean
        stat[layer, i, 0] = jnp.broadcast_to(mean, (rows, BLOCK))
        stat[layer, i, 1] = jnp.broadcast_to(jnp.sum(centered * centered, axis=1, keepdims=True), (rows, BLOCK))
        swap_stat(layer, i).start()

    def renew_done(layer, i):
        swap_stat(layer, i).wait()
        mean, other_mean = stat[layer, i, 0][:, :1], stat_in[layer, i, 0][:, :1]
        apart = mean - other_mean
        var = (stat[layer, i, 1][:, :1] + stat_in[layer, i, 1][:, :1] + apart * apart * (half / 2)) / width
        acts[layer, me_o, zi, i] = (
            (state[i].astype(jnp.float32) - (mean + other_mean) * 0.5) * lax.rsqrt(var + 1e-05)
            * gains_ref[pl.ds(layer, 1), mine]).astype(jnp.bfloat16)

    def sublayer(layer, carry):
        @pl.when(hi == layer)
        def _():
            logs["plane"] = plane(layer)

        @pl.when(hi != layer)
        def _():
            logs["beside"] = beside(layer)

        return carry

    lax.fori_loop(0, LAYERS, sublayer, 0)

    last = remote(state.at[1 - core], out_in, osem.at[0], osem.at[1], p_dev)
    last.start()
    out_ref[:, mine] = state[core]
    for name, layer in (("plane", hi), ("beside", 1 - hi)):
        for send, cond in logs[name]:
            when(cond(), lambda send=send, layer=layer: remote(
                out_in, out_in, send(layer), osem.at[1], x_dev).wait_send())
    for n in range(len(blocks)):
        for g in range(owners):
            give(n, g).wait_send()
    for g in range(owners):
        swap_pre(g).wait_send()
    swap_normed.wait_send()
    swap_state.wait_send()
    last.wait()
    out_ref[:, theirs] = out_in[...]


def scratch_plan(owners, batches, rows, width):
    zn = batches // CORES
    half = width // CORES
    bf, full = jnp.bfloat16, jnp.float32
    shard = (CORES, rows, half)
    return [
        (shard, bf),
        ((LAYERS, owners, zn) + shard, bf),
        ((owners, CORES, BLOCK, half), bf),
        ((owners, CORES, BLOCK, half), bf),
        ((owners, batches * rows, CORES * BLOCK), full),
        ((owners, batches * rows, CORES * BLOCK), full),
        ((owners, zn) + shard, bf),
        ((zn + 1,) + shard, bf),
        ((zn + 1,) + shard, bf),
        (shard, bf),
        ((LAYERS, zn + 1) + shard, bf),
        ((zn,) + shard, bf),
        ((LAYERS, CORES, 2, rows, BLOCK), full),
        ((LAYERS, CORES, 2, rows, BLOCK), full),
        ((rows, half), bf),
        ((rows, half), full),
        ((rows, width), bf),
    ]


def scratch_bytes(plan):
    total = 0
    for shape, kind in plan:
        size = jnp.dtype(kind).itemsize
        for extent in shape:
            size *= extent
        total += size
    return total


def run_sublayers(owners, batches, hidden, gains, live, up_send, down_send):
    rows, width = hidden.shape
    zn = batches // CORES
    plan = scratch_plan(owners, batches, rows, width)
    dma = pltpu.SemaphoreType.DMA
    sems = [
        (2, 3, owners), (4,), (2,), (2, LAYERS, CORES), (2, owners), (LAYERS, owners, zn, CORES),
        (LAYERS, 2 * zn, CORES), (LAYERS, 2 * zn, CORES), (LAYERS, 2 * zn, CORES), (LAYERS, 2 * zn, CORES),
        (2 * zn + 1, CORES), (2 * zn, CORES), (LAYERS, 2 * zn, CORES), (LAYERS, 2 * zn, CORES),
        (zn + 1, CORES), (zn + 1, CORES), (CORES,), (LAYERS, zn + 1, CORES), (zn, CORES),
    ]
    vmem = pl.BlockSpec(memory_space=pltpu.VMEM)
    hbm = pl.BlockSpec(memory_space=pl.ANY)
    return pl.pallas_call(
        functools.partial(sublayers_kernel, owners, batches),
        out_shape=jax.ShapeDtypeStruct((rows, width), jnp.bfloat16),
        in_specs=[vmem] * 5,
        out_specs=vmem,
        scratch_shapes=[pltpu.VMEM(s, d) for s, d in plan] + [dma(s) for s in sems],
        compiler_params=pltpu.CompilerParams(
            collective_id=0, has_side_effects=True, vmem_limit_bytes=VMEM_BUDGET),
        name="sublayers",
    )(hidden, gains, live, up_send, down_send)


def fetch_kernel(owners, batches, held, pick_ref, up_ref, down_ref, live_ref, up_out, down_out, sem):
    sender = lax.axis_index("owner") * batches + lax.axis_index("batch")

    def read(i):
        g = i % owners
        at = jnp.minimum(pick_ref[g, sender], held - 1)
        src, dst = (up_ref, up_out) if i < owners else (down_ref, down_out)
        return pltpu.make_async_copy(src.at[at], dst.at[g], sem.at[i])

    for i in range(2 * owners):
        read(i).start()
    first = sender - sender % CORES
    for g in range(owners):
        for n in range(CORES):
            live = (pick_ref[g, first + n] < held).astype(jnp.float32)
            live_ref[g:g + 1, n * BLOCK:(n + 1) * BLOCK] = jnp.full((1, BLOCK), live, jnp.float32)
    for i in range(2 * owners):
        read(i).wait()


def fetch(owners, batches, up_rows, down_rows, pick, near):
    width = up_rows.shape[1]
    held = up_rows.shape[0] // BLOCK
    hbm = pl.BlockSpec(memory_space=pl.ANY)
    vmem = pl.BlockSpec(memory_space=pltpu.VMEM)
    shape = (owners, BLOCK, width)
    sent = pltpu.VMEM(shape, up_rows.dtype) if near else jax.ShapeDtypeStruct(shape, up_rows.dtype)
    return pl.pallas_call(
        functools.partial(fetch_kernel, owners, batches, held),
        out_shape=(jax.ShapeDtypeStruct((owners, CORES * BLOCK), jnp.float32), sent, sent),
        in_specs=[pl.BlockSpec(memory_space=pltpu.SMEM), hbm, hbm],
        out_specs=(vmem, vmem, vmem) if near else (vmem, hbm, hbm),
        scratch_shapes=[pltpu.SemaphoreType.DMA((2 * owners,))],
        compiler_params=pltpu.CompilerParams(vmem_limit_bytes=FETCH_BUDGET),
        name="fetch",
    )(pick, up_rows.reshape(held, BLOCK, width), down_rows.reshape(held, BLOCK, width))


def stay_body(hidden, gains, up_rows, down_rows, pick):
    owners = lax.axis_size("owner")
    batches = lax.axis_size("batch")
    live, up_send, down_send = fetch(owners, batches, up_rows, down_rows, pick, True)
    return run_sublayers(owners, batches, hidden, gains, live, up_send, down_send)


def normalize(rows_in, gain_row):
    values = rows_in.astype(jnp.float32)
    row_mean = jnp.mean(values, axis=1, keepdims=True)
    centered = values - row_mean
    row_var = jnp.mean(centered * centered, axis=1, keepdims=True)
    return (centered * lax.rsqrt(row_var + 1e-05) * gain_row[None, :]).astype(jnp.bfloat16)


def body(hidden, gains, up_rows, down_rows, pick):
    owners = lax.axis_size("owner")
    batches = lax.axis_size("batch")
    group_at = lax.axis_index("owner")
    lane_at = lax.axis_index("batch")
    held_blocks = up_rows.shape[0] // BLOCK
    model_width = up_rows.shape[1]
    local_rows = hidden.shape[0]
    _, up_send, down_send = fetch(owners, batches, up_rows, down_rows, pick, False)
    group_picks = lax.dynamic_slice_in_dim(pick, group_at, 1, 0)[0]
    live_slots = (group_picks[jnp.arange(owners) * batches + lane_at] < held_blocks).astype(
        jnp.float32
    )
    up_recv, down_recv = (
        lax.all_to_all(up_send, "owner", split_axis=0, concat_axis=0, tiled=True),
        lax.all_to_all(down_send, "owner", split_axis=0, concat_axis=0, tiled=True),
    )
    per_layer = owners // LAYERS
    residual = hidden
    for layer_at in range(LAYERS):
        first_slot = layer_at * per_layer
        up_part = up_recv[first_slot : first_slot + per_layer]
        down_part = down_recv[first_slot : first_slot + per_layer]
        keep_slots = live_slots[first_slot : first_slot + per_layer]
        up_flat = up_part.reshape(per_layer * BLOCK, model_width)
        down_flat = down_part.reshape(per_layer * BLOCK, model_width)
        neuron_mask = jnp.repeat(keep_slots, BLOCK)
        normed = normalize(residual, gains[layer_at])

        def expand(
            rows_piece,
            row_start,
            up_part=up_part,
            up_flat=up_flat,
            keep_slots=keep_slots,
            neuron_mask=neuron_mask,
        ):
            pre_act = lax.dot_general(
                rows_piece, up_flat, (((1,), (1,)), ((), ())), preferred_element_type=jnp.float32
            )
            return (jnp.maximum(pre_act, 0.0) * neuron_mask[None, :]).astype(jnp.bfloat16)

        active = expand(lax.all_gather(normed, "batch", axis=0, tiled=True), jnp.int32(0))

        def contract(
            row_start,
            row_count,
            active=active,
            down_part=down_part,
            down_flat=down_flat,
            keep_slots=keep_slots,
        ):
            return jnp.dot(active, down_flat, preferred_element_type=jnp.float32)

        summed = lax.psum_scatter(
            contract(jnp.int32(0), lax.axis_size("batch") * local_rows).astype(jnp.bfloat16),
            "batch",
            scatter_dimension=0,
            tiled=True,
        ).astype(jnp.float32)
        residual = (residual.astype(jnp.float32) + summed).astype(jnp.bfloat16)
    return residual


def solution(mesh):
    in_specs = (
        P(("owner", "batch"), None),
        P(),
        P(("owner", "batch"), None),
        P(("owner", "batch"), None),
        P(),
    )
    out_specs = P(("owner", "batch"), None)
    owners, batches = mesh.shape["owner"], mesh.shape["batch"]

    def whole(hidden, gains, up_rows, down_rows, pick):
        rows = hidden.shape[0] // (owners * batches)
        plan = scratch_plan(owners, batches, rows, hidden.shape[1])
        line = batches == 2 * TWINS * CORES
        fits = line and owners == 2 * LAYERS and scratch_bytes(plan) * 5 < VMEM_BUDGET * 4
        chosen = stay_body if fits else body
        return jax.shard_map(chosen, mesh=mesh, in_specs=in_specs, out_specs=out_specs, check_vma=False)(
            hidden, gains, up_rows, down_rows, pick)

    return whole
```

```python
import functools

import jax
import jax.numpy as jnp
from jax import lax
from jax.experimental import pallas as pl
from jax.experimental.pallas import tpu as pltpu
from jax.sharding import PartitionSpec as P

BLOCK = 128
LAYERS = 2
CORES = 2
TWINS = 2
VMEM_BUDGET = 40 * 1024 * 1024
FETCH_BUDGET = 40 * 1024 * 1024
CHUNK = 1024


def sublayers_kernel(
    owners, batches,
    hidden_ref, gains_ref, live_ref, up_hbm, down_hbm, out_ref,
    state, acts, up_v, down_v, pre, pre_in, part, x_in, y_in, q_in, z_in, r_in, stat, stat_in, out_in, total, normed,
    wsem, hsem, osem, ssem, pre_sem, ag_recv, x_send, y_send, up_send, dn_send,
    rx_send, ry_send, rup_send, rdn_send, x_recv, y_recv, q_recv, z_recv, r_recv,
):
    zn = batches // CORES
    per_layer = owners // LAYERS
    rows, width = hidden_ref.shape
    half = width // CORES
    group_rows = batches * rows
    me_o = lax.axis_index("owner")
    me_b = lax.axis_index("batch")
    hi, lo = me_o // per_layer, me_o % per_layer
    zi, core = me_b // CORES, me_b % CORES
    other = 1 - core
    peer_x = hi * per_layer + (1 - lo)
    peer_y = (1 - hi) * per_layer + lo
    diag = (1 - hi) * per_layer + (1 - lo)
    x_dev, y_dev = (peer_x, me_b), (peer_y, me_b)
    p_dev = (me_o, zi * CORES + 1 - core)
    up_dev, dn_dev = (me_o, me_b + CORES), (me_o, me_b - CORES)
    has_up, has_dn = zi < zn - 1, zi > 0
    lower = zi < zn // 2
    upper = zi >= zn // 2
    low = lower.astype(jnp.int32)
    twin = zi + 1 - 2 * (zi % 2)
    inner = jnp.logical_and(zi > 0, zi < zn - 1)
    outer = jnp.logical_not(inner)
    inner_lower, inner_upper = jnp.logical_and(inner, lower), jnp.logical_and(inner, upper)
    mine = pl.ds(pl.multiple_of(core * half, 128), half)
    theirs = pl.ds(pl.multiple_of((1 - core) * half, 128), half)
    parts = range(CORES)

    def remote(src, dst, send, recv, dev):
        return pltpu.make_async_remote_copy(
            src_ref=src, dst_ref=dst, send_sem=send, recv_sem=recv,
            device_id=dev, device_id_type=pl.DeviceIdType.MESH)

    def always():
        return True

    def when(cond, run):
        if cond is True:
            run()
        else:
            pl.when(cond)(run)

    barrier = pltpu.get_barrier_semaphore()
    for cond, dev in ((True, x_dev), (True, y_dev), (True, p_dev), (has_up, up_dev), (has_dn, dn_dev)):
        when(cond, lambda dev=dev: pl.semaphore_signal(
            barrier, inc=1, device_id=dev, device_id_type=pl.DeviceIdType.MESH))
    normed[...] = normalize(hidden_ref[...], gains_ref[0])
    acts[0, me_o, zi, core] = normed[:, mine]
    state[core] = hidden_ref[:, mine]
    pl.semaphore_wait(barrier, 3 + has_up.astype(jnp.int32) + has_dn.astype(jnp.int32))

    swap_normed = remote(normed.at[:, theirs], acts.at[0, me_o, zi, core], hsem.at[0], hsem.at[1], p_dev)
    swap_state = remote(hidden_ref.at[:, theirs], state.at[core], hsem.at[2], hsem.at[3], p_dev)
    swap_normed.start()
    swap_state.start()

    blocks = ((up_hbm, up_v), (down_hbm, down_v))

    def keep(n, g):
        hbm, vmem = blocks[n]
        return pltpu.make_async_copy(hbm.at[g, :, mine], vmem.at[g, core], wsem.at[n, 0, g])

    def give(n, g):
        hbm, vmem = blocks[n]
        return remote(hbm.at[g, :, theirs], vmem.at[g, core], wsem.at[n, 1, g], wsem.at[n, 2, g], p_dev)

    def wait_weight(n, g):
        keep(n, g).wait()
        give(n, g).wait_recv()

    class Sender:
        def __init__(self, layer):
            self.layer, self.log, self.mute = layer, [], False

        def go(self, src, dst, send, recv, dev, cond=always):
            when(cond(), lambda: remote(src, dst, send(self.layer), recv, dev).start())
            if not self.mute:
                self.log.append((send, cond))

        def flush(self):
            for send, cond in self.log:
                when(cond(), lambda send=send: remote(
                    out_in, out_in, send(self.layer), osem.at[1], x_dev).wait_send())
            self.log.clear()

        def spread_piece(self, sems, g, j, i, slot, dev, cond):
            ref = acts.at[self.layer, g, j, i]
            self.go(ref, ref, lambda layer: sems.at[layer, slot, i], ag_recv.at[self.layer, g, j, i], dev, cond)

        def x(self, g, j, i, slot, cond=always):
            self.spread_piece(x_send, g, j, i, slot, x_dev, cond)

        def y(self, g, j, i, slot, cond=always):
            self.spread_piece(y_send, g, j, i, slot, y_dev, cond)

        def up(self, g, j, i, slot, cond):
            self.spread_piece(up_send, g, j, i, slot, up_dev, cond)

        def dn(self, g, j, i, slot, cond):
            self.spread_piece(dn_send, g, j, i, slot, dn_dev, cond)

    def arrive(layer, g, j, i):
        ref = acts.at[layer, g, j, i]
        remote(ref, ref, x_send.at[0, 0, 0], ag_recv.at[layer, g, j, i], x_dev).wait_recv()

    def below(k):
        return lambda: zi - k >= 0

    def above(k):
        return lambda: zi + k < zn

    def column(t, k, i):
        for j, there, send, more in ((zi - k, below(k), t.up, has_up), (zi + k, above(k), t.dn, has_dn)):
            when(there(), lambda j=j: arrive(t.layer, me_o, j, i))
            if k < zn - 1:
                send(me_o, j, i, k, lambda there=there, more=more: jnp.logical_and(there(), more))

    def across(send, k, i):
        send(me_o, zi - k, i, k, below(k))
        send(me_o, zi + k, i, zn - 1 + k, above(k))

    def combine(dst, terms):
        total = dst[...].astype(jnp.float32)
        for term in terms:
            total = total + term[...].astype(jnp.float32)
        dst[...] = total.astype(jnp.bfloat16)

    def line(t, col, k, i, fold):
        for j, there, slot, behind, sends, dev in (
            (zi + k, above(k), zi + k, has_dn, rup_send, up_dev),
            (zi - k, below(k), zn if k == 1 else zi - k, has_up, rdn_send, dn_dev),
        ):
            @pl.when(there())
            def _(j=j, behind=behind):
                fold(j, i, k)

                @pl.when(behind)
                def _():
                    z_wait(t.layer, j, i)
                    combine(col(j, i), [z_in.at[t.layer, j, i]])

            t.go(col(j, i), z_in.at[t.layer, slot, i], lambda layer, sends=sends: sends.at[layer, k, i],
                 z_recv.at[t.layer, slot, i], dev, there)

    def z_wait(layer, slot, i):
        ref = z_in.at[layer, slot, i]
        remote(ref, ref, rup_send.at[0, 0, 0], z_recv.at[layer, slot, i], up_dev).wait_recv()

    def home(layer, col, i, fold):
        fold(zi, i, 0)
        total[...] = state[i].astype(jnp.float32) + col(zi, i)[...].astype(jnp.float32)
        for cond, slot in ((has_dn, zi), (has_up, zn)):
            @pl.when(cond)
            def _(slot=slot):
                z_wait(layer, slot, i)
                total[...] = total[...] + z_in[layer, slot, i].astype(jnp.float32)

        state[i] = total[...].astype(jnp.bfloat16)

        @pl.when(layer < LAYERS - 1)
        def _():
            renew(layer + 1, i)

    def hidden_sum(layer, g):
        wait_weight(0, g)
        flat = acts[layer, g].reshape(group_rows, half)
        pre[g] = lax.dot_general(
            flat, up_v[g].reshape(CORES * BLOCK, half), (((1,), (1,)), ((), ())), preferred_element_type=jnp.float32)
        swap_pre(g).start()

    def swap_pre(g):
        return remote(pre.at[g], pre_in.at[g], pre_sem.at[0, g], pre_sem.at[1, g], p_dev)

    def spread(g):
        wait_weight(1, g)
        swap_pre(g).wait_recv()
        both = pre[g] + pre_in[g]
        active = (jnp.maximum(both, 0.0) * live_ref[pl.ds(g, 1), :]).astype(jnp.bfloat16)
        for at in range(0, half, CHUNK):
            cols = pl.ds(at, min(CHUNK, half - at))
            made = jnp.dot(active, down_v[g, :, :, cols].reshape(CORES * BLOCK, -1), preferred_element_type=jnp.float32)
            part[g, :, :, :, cols] = made.astype(jnp.bfloat16).reshape(zn, CORES, rows, -1)

    def opening(t, toward, sems):
        def out(i):
            toward(me_o, zi, i, 0)
            t.up(me_o, zi, i, 0, lambda: has_up)
            t.dn(me_o, zi, i, 0, lambda: has_dn)

        t.mute = True

        @pl.when(t.layer == 0)
        def _():
            out(core)
            swap_normed.wait_recv()
            out(other)
            for n in range(len(blocks)):
                for g in range(owners):
                    keep(n, g).start()
                    give(n, g).start()
            swap_state.wait()
            swap_normed.wait_send()

        @pl.when(t.layer > 0)
        def _():
            for i in parts:
                renew_done(t.layer, i)
                out(i)

        t.mute = False
        for i in parts:
            for used, cond in ((sems, always), (up_send, lambda: has_up), (dn_send, lambda: has_dn)):
                t.log.append((lambda layer, used=used, i=i: used.at[layer, 0, i], cond))

    def plane(layer):
        t = Sender(layer)
        opening(t, t.x, x_send)
        far = [low * (zn // 2 + n) + (1 - low) * (zn // 2 - 1 - n) for n in range(zn // 2)]

        def is_inner():
            return inner

        def is_outer():
            return outer

        def at_inner(g, j, i):
            when(inner, lambda: arrive(layer, g, j, i))

        def at_outer(g, j, i):
            when(outer, lambda: arrive(layer, g, j, i))

        def diagonal(j, i, slot):
            at_inner(diag, j, i)
            t.up(diag, j, i, slot, lambda: inner_lower)
            t.dn(diag, j, i, slot, lambda: inner_upper)

        def relay(n, i):
            at_inner(diag, far[n], i)
            t.dn(diag, far[n], i, zn - 1 + n, lambda: inner_lower)
            t.up(diag, far[n], i, zn - 1 + n, lambda: inner_upper)

        for i in parts:
            at_inner(peer_y, zi, i)
            t.x(peer_y, zi, i, 2 * zn - 1, is_inner)
            column(t, 1, i)
        for i in parts:
            across(t.x, 1, i)
        for i in parts:
            diagonal(zi, i, zn - 1)
            column(t, 2, i)
            across(t.x, 2, i)
        for i in parts:
            diagonal(twin, i, zn)
            for k in range(3, zn):
                column(t, k, i)
                across(t.x, k, i)
            relay(0, i)
        for i in parts:
            at_outer(peer_y, zi, i)
            t.x(peer_y, zi, i, 2 * zn - 1, is_outer)
        hidden_sum(layer, me_o)
        for n in range(1, zn // 2):
            for i in parts:
                relay(n, i)
        spread(me_o)

        def away(k):
            return ((zi + k, above(k), k), (zi - k, below(k), zn - 1 + k))

        def give_x(g, j, i, slot, to, cond=always):
            t.go(part.at[g, j, i], x_in.at[to, i], lambda layer: rx_send.at[slot, i], x_recv.at[to, i], x_dev, cond)

        def give_y(g, j, i, slot, to, cond=always):
            t.go(part.at[g, j, i], y_in.at[to, i], lambda layer: ry_send.at[slot, i], y_recv.at[to, i], y_dev, cond)

        def relay_wait(j, i):
            ref = r_in.at[j, i]
            remote(ref, ref, rup_send.at[0, 0, 0], r_recv.at[j, i], up_dev).wait_recv()

        def relayed(j, i):
            @pl.when(inner)
            def _():
                relay_wait(j, i)
                combine(part.at[diag, j, i], [r_in.at[j, i]])

        def give_z(n, i, place):
            for sends, dev, side in ((rup_send, up_dev, lower), (rdn_send, dn_dev, upper)):
                t.go(part.at[diag, far[n], i], r_in.at[far[n], i],
                     lambda layer, sends=sends: sends.at[layer, zn + n, i],
                     r_recv.at[far[n], i], dev, lambda side=side: jnp.logical_and(side, place))

        def relay_in(n, i):
            relayed(far[n], i)
            give_z(n, i, inner)

        def col(j, i):
            return part.at[me_o, j, i]

        def x_wait(slot, i):
            ref = x_in.at[slot, i]
            remote(ref, ref, rx_send.at[0, 0], x_recv.at[slot, i], x_dev).wait_recv()

        def fold(j, i, k):
            x_wait(j, i)
            combine(col(j, i), [x_in.at[j, i]])

        gathered, t = t, Sender(layer)

        def wait_x():
            for j in range(zn):
                for i in parts:
                    arrive(layer, peer_x, j, i)

        def wait_y():
            for k in range(1, zn):
                for j, there in ((zi - k, below(k)), (zi + k, above(k))):
                    for i in parts:
                        when(there(), lambda j=j, i=i: arrive(layer, peer_y, j, i))

        def wait_diag():
            for j in [zi, twin] + far:
                for i in parts:
                    arrive(layer, diag, j, i)

        def send_x(place):
            for k in range(zn - 1, 0, -1):
                for j, there, slot in away(k):
                    for i in parts:
                        give_x(peer_x, j, i, slot, j, lambda there=there: jnp.logical_and(there(), place))

        def send_y(place):
            for k in range(zn - 1, 1, -1):
                for j, there, slot in away(k):
                    for i in parts:
                        give_y(peer_y, j, i, slot, j, lambda there=there: jnp.logical_and(there(), place))

        inside = inner.astype(jnp.int32)

        def either(at_in, at_out):
            return inside * at_in + (1 - inside) * at_out

        when(outer, wait_x)
        hidden_sum(layer, either(diag, peer_x))
        when(inner, wait_x)
        when(outer, wait_y)
        hidden_sum(layer, either(peer_x, peer_y))
        spread(either(diag, peer_x))
        send_x(outer)
        when(outer, lambda: spread(peer_y))
        send_y(outer)
        when(outer, wait_diag)
        when(inner, wait_y)
        hidden_sum(layer, either(peer_y, diag))
        when(inner, lambda: spread(peer_x))
        send_x(inner)
        spread(either(peer_y, diag))
        for n in reversed(range(zn // 2)):
            for i in parts:
                give_z(n, i, outer)
        send_y(inner)
        for i in parts:
            give_y(peer_y, 2 * zi - twin, i, 1, 2 * zi - twin, lambda: inner)
        gathered.flush()
        for g in range(owners):
            swap_pre(g).wait_send()
            for n in range(len(blocks)):
                give(n, g).wait_send()
        for n in reversed(range(1, zn // 2)):
            for i in parts:
                relay_in(n, i)
        for i in parts:
            relay_in(0, i)
            for k in range(zn - 1, 2, -1):
                line(t, col, k, i, fold)
            relayed(twin, i)
            give_y(diag, twin, i, 2 * zn - 1, zn)
        for i in parts:
            give_y(peer_y, twin, i, zn, twin)
        for i in parts:
            relayed(zi, i)
            give_x(diag, zi, i, 2 * zn - 1, zn)
            line(t, col, 2, i, fold)
        for i in parts:
            give_x(peer_x, zi, i, 0, zi)
        for i in parts:
            line(t, col, 1, i, fold)
            x_wait(zn, i)
            combine(part.at[peer_y, zi, i], [x_in.at[zn, i]])
            give_y(peer_y, zi, i, 0, zi)
        for i in parts:
            home(layer, col, i, fold)
            if i == 0:
                t.flush()

    def beside(layer):
        t = Sender(layer)
        opening(t, t.y, y_send)

        def beyond(send, i, near):
            for sign, slot in ((-1, 1), (1, zn)):
                send(me_o, zi + sign, i, slot, lambda sign=sign: (
                    zi + sign == twin if near else jnp.logical_and(inner, zi + sign != twin)))

        for i in parts:
            column(t, 1, i)
            beyond(t.x, i, True)
        for i in parts:
            beyond(t.y, i, True)
        for i in parts:
            when(inner, lambda i=i: arrive(layer, peer_x, twin, i))
            t.y(peer_x, twin, i, 2 * zn - 1, lambda: inner)
            column(t, 2, i)
        for i in parts:
            beyond(t.y, i, False)
        for i in parts:
            across(t.y, 2, i)
        for k in range(3, zn):
            for i in parts:
                column(t, k, i)
                across(t.y, k, i)
        for i in parts:
            when(outer, lambda i=i: arrive(layer, peer_x, twin, i))
            t.y(peer_x, twin, i, 2 * zn - 1, lambda: outer)

        t.flush()

        def col(j, i):
            return y_in.at[j, i]

        def y_wait(slot, i):
            ref = y_in.at[slot, i]
            remote(ref, ref, ry_send.at[0, 0], y_recv.at[slot, i], y_dev).wait_recv()

        def fold(j, i, k):
            y_wait(j, i)
            if k == 1:
                @pl.when(j == twin)
                def _():
                    remote(q_in.at[i], q_in.at[i], rx_send.at[2 * zn, i], q_recv.at[i], x_dev).wait_recv()
                    combine(col(j, i), [q_in.at[i]])

        for k in range(zn - 1, 1, -1):
            for i in parts:
                line(t, col, k, i, fold)
        for i in parts:
            y_wait(zn, i)
            t.go(y_in.at[zn, i], q_in.at[i], lambda layer, i=i: rx_send.at[2 * zn, i], q_recv.at[i], x_dev)
        for i in parts:
            line(t, col, 1, i, fold)
        for i in parts:
            home(layer, col, i, fold)
            if i == 0:
                t.flush()

    def swap_stat(layer, i):
        return remote(stat.at[layer, i], stat_in.at[layer, i], ssem.at[0, layer, i], ssem.at[1, layer, i], p_dev)

    def renew(layer, i):
        values = state[i].astype(jnp.float32)
        mean = jnp.sum(values, axis=1, keepdims=True) / half
        centered = values - mean
        stat[layer, i, 0] = jnp.broadcast_to(mean, (rows, BLOCK))
        stat[layer, i, 1] = jnp.broadcast_to(jnp.sum(centered * centered, axis=1, keepdims=True), (rows, BLOCK))
        swap_stat(layer, i).start()

    def renew_done(layer, i):
        swap_stat(layer, i).wait()
        mean, other_mean = stat[layer, i, 0][:, :1], stat_in[layer, i, 0][:, :1]
        apart = mean - other_mean
        var = (stat[layer, i, 1][:, :1] + stat_in[layer, i, 1][:, :1] + apart * apart * (half / 2)) / width
        acts[layer, me_o, zi, i] = (
            (state[i].astype(jnp.float32) - (mean + other_mean) * 0.5) * lax.rsqrt(var + 1e-05)
            * gains_ref[pl.ds(layer, 1), mine]).astype(jnp.bfloat16)

    def sublayer(layer, carry):
        @pl.when(hi == layer)
        def _():
            plane(layer)

        @pl.when(hi != layer)
        def _():
            beside(layer)

        return carry

    lax.fori_loop(0, LAYERS, sublayer, 0)

    last = remote(state.at[1 - core], out_in, osem.at[0], osem.at[1], p_dev)
    last.start()
    out_ref[:, mine] = state[core]
    last.wait()
    out_ref[:, theirs] = out_in[...]


def scratch_plan(owners, batches, rows, width):
    zn = batches // CORES
    half = width // CORES
    bf, full = jnp.bfloat16, jnp.float32
    shard = (CORES, rows, half)
    return [
        (shard, bf),
        ((LAYERS, owners, zn) + shard, bf),
        ((owners, CORES, BLOCK, half), bf),
        ((owners, CORES, BLOCK, half), bf),
        ((owners, batches * rows, CORES * BLOCK), full),
        ((owners, batches * rows, CORES * BLOCK), full),
        ((owners, zn) + shard, bf),
        ((zn + 1,) + shard, bf),
        ((zn + 1,) + shard, bf),
        (shard, bf),
        ((LAYERS, zn + 1) + shard, bf),
        ((zn,) + shard, bf),
        ((LAYERS, CORES, 2, rows, BLOCK), full),
        ((LAYERS, CORES, 2, rows, BLOCK), full),
        ((rows, half), bf),
        ((rows, half), full),
        ((rows, width), bf),
    ]


def scratch_bytes(plan):
    total = 0
    for shape, kind in plan:
        size = jnp.dtype(kind).itemsize
        for extent in shape:
            size *= extent
        total += size
    return total


def run_sublayers(owners, batches, hidden, gains, live, up_send, down_send):
    rows, width = hidden.shape
    zn = batches // CORES
    plan = scratch_plan(owners, batches, rows, width)
    dma = pltpu.SemaphoreType.DMA
    sems = [
        (2, 3, owners), (4,), (2,), (2, LAYERS, CORES), (2, owners), (LAYERS, owners, zn, CORES),
        (LAYERS, 2 * zn, CORES), (LAYERS, 2 * zn, CORES), (LAYERS, 2 * zn, CORES), (LAYERS, 2 * zn, CORES),
        (2 * zn + 1, CORES), (2 * zn, CORES), (LAYERS, 2 * zn, CORES), (LAYERS, 2 * zn, CORES),
        (zn + 1, CORES), (zn + 1, CORES), (CORES,), (LAYERS, zn + 1, CORES), (zn, CORES),
    ]
    vmem = pl.BlockSpec(memory_space=pltpu.VMEM)
    hbm = pl.BlockSpec(memory_space=pl.ANY)
    return pl.pallas_call(
        functools.partial(sublayers_kernel, owners, batches),
        out_shape=jax.ShapeDtypeStruct((rows, width), jnp.bfloat16),
        in_specs=[vmem] * 5,
        out_specs=vmem,
        scratch_shapes=[pltpu.VMEM(s, d) for s, d in plan] + [dma(s) for s in sems],
        compiler_params=pltpu.CompilerParams(
            collective_id=0, has_side_effects=True, vmem_limit_bytes=VMEM_BUDGET),
        name="sublayers",
    )(hidden, gains, live, up_send, down_send)


def fetch_kernel(owners, batches, held, pick_ref, up_ref, down_ref, live_ref, up_out, down_out, sem):
    sender = lax.axis_index("owner") * batches + lax.axis_index("batch")

    unit = lax.broadcasted_iota(jnp.int32, (1, pick_ref.shape[1]), 1)

    def picked(g, at):
        return jnp.sum(jnp.where(unit == at, pick_ref[g:g + 1, :], 0))

    chosen = [jnp.minimum(picked(g, sender), held - 1) for g in range(owners)]

    def read(i):
        g = i % owners
        src, dst = (up_ref, up_out) if i < owners else (down_ref, down_out)
        return pltpu.make_async_copy(src.at[chosen[g]], dst.at[g], sem.at[i])

    copies = [read(i) for i in range(2 * owners)]
    for copy in copies:
        copy.start()
    first = sender - sender % CORES
    for g in range(owners):
        for n in range(CORES):
            live = (picked(g, first + n) < held).astype(jnp.float32)
            live_ref[g:g + 1, n * BLOCK:(n + 1) * BLOCK] = jnp.full((1, BLOCK), live, jnp.float32)
    for copy in copies:
        copy.wait()


def fetch(owners, batches, up_rows, down_rows, pick, near):
    width = up_rows.shape[1]
    held = up_rows.shape[0] // BLOCK
    hbm = pl.BlockSpec(memory_space=pl.ANY)
    vmem = pl.BlockSpec(memory_space=pltpu.VMEM)
    shape = (owners, BLOCK, width)
    sent = pltpu.VMEM(shape, up_rows.dtype) if near else jax.ShapeDtypeStruct(shape, up_rows.dtype)
    return pl.pallas_call(
        functools.partial(fetch_kernel, owners, batches, held),
        out_shape=(jax.ShapeDtypeStruct((owners, CORES * BLOCK), jnp.float32), sent, sent),
        in_specs=[vmem, hbm, hbm],
        out_specs=(vmem, vmem, vmem) if near else (vmem, hbm, hbm),
        scratch_shapes=[pltpu.SemaphoreType.DMA((2 * owners,))],
        compiler_params=pltpu.CompilerParams(vmem_limit_bytes=FETCH_BUDGET),
        name="fetch",
    )(pick, up_rows.reshape(held, BLOCK, width), down_rows.reshape(held, BLOCK, width))


def stay_body(hidden, gains, up_rows, down_rows, pick):
    owners = lax.axis_size("owner")
    batches = lax.axis_size("batch")
    live, up_send, down_send = fetch(owners, batches, up_rows, down_rows, pick, True)
    return run_sublayers(owners, batches, hidden, gains, live, up_send, down_send)


def normalize(rows_in, gain_row):
    values = rows_in.astype(jnp.float32)
    row_mean = jnp.mean(values, axis=1, keepdims=True)
    centered = values - row_mean
    row_var = jnp.mean(centered * centered, axis=1, keepdims=True)
    return (centered * lax.rsqrt(row_var + 1e-05) * gain_row[None, :]).astype(jnp.bfloat16)


def body(hidden, gains, up_rows, down_rows, pick):
    owners = lax.axis_size("owner")
    batches = lax.axis_size("batch")
    group_at = lax.axis_index("owner")
    lane_at = lax.axis_index("batch")
    held_blocks = up_rows.shape[0] // BLOCK
    model_width = up_rows.shape[1]
    local_rows = hidden.shape[0]
    _, up_send, down_send = fetch(owners, batches, up_rows, down_rows, pick, False)
    group_picks = lax.dynamic_slice_in_dim(pick, group_at, 1, 0)[0]
    live_slots = (group_picks[jnp.arange(owners) * batches + lane_at] < held_blocks).astype(
        jnp.float32
    )
    up_recv, down_recv = (
        lax.all_to_all(up_send, "owner", split_axis=0, concat_axis=0, tiled=True),
        lax.all_to_all(down_send, "owner", split_axis=0, concat_axis=0, tiled=True),
    )
    per_layer = owners // LAYERS
    residual = hidden
    for layer_at in range(LAYERS):
        first_slot = layer_at * per_layer
        up_part = up_recv[first_slot : first_slot + per_layer]
        down_part = down_recv[first_slot : first_slot + per_layer]
        keep_slots = live_slots[first_slot : first_slot + per_layer]
        up_flat = up_part.reshape(per_layer * BLOCK, model_width)
        down_flat = down_part.reshape(per_layer * BLOCK, model_width)
        neuron_mask = jnp.repeat(keep_slots, BLOCK)
        normed = normalize(residual, gains[layer_at])

        def expand(
            rows_piece,
            row_start,
            up_part=up_part,
            up_flat=up_flat,
            keep_slots=keep_slots,
            neuron_mask=neuron_mask,
        ):
            pre_act = lax.dot_general(
                rows_piece, up_flat, (((1,), (1,)), ((), ())), preferred_element_type=jnp.float32
            )
            return (jnp.maximum(pre_act, 0.0) * neuron_mask[None, :]).astype(jnp.bfloat16)

        active = expand(lax.all_gather(normed, "batch", axis=0, tiled=True), jnp.int32(0))

        def contract(
            row_start,
            row_count,
            active=active,
            down_part=down_part,
            down_flat=down_flat,
            keep_slots=keep_slots,
        ):
            return jnp.dot(active, down_flat, preferred_element_type=jnp.float32)

        summed = lax.psum_scatter(
            contract(jnp.int32(0), lax.axis_size("batch") * local_rows).astype(jnp.bfloat16),
            "batch",
            scatter_dimension=0,
            tiled=True,
        ).astype(jnp.float32)
        residual = (residual.astype(jnp.float32) + summed).astype(jnp.bfloat16)
    return residual


def solution(mesh):
    in_specs = (
        P(("owner", "batch"), None),
        P(),
        P(("owner", "batch"), None),
        P(("owner", "batch"), None),
        P(),
    )
    out_specs = P(("owner", "batch"), None)
    owners, batches = mesh.shape["owner"], mesh.shape["batch"]

    def whole(hidden, gains, up_rows, down_rows, pick):
        rows = hidden.shape[0] // (owners * batches)
        plan = scratch_plan(owners, batches, rows, hidden.shape[1])
        line = batches == 2 * TWINS * CORES
        fits = line and owners == 2 * LAYERS and scratch_bytes(plan) * 5 < VMEM_BUDGET * 4
        chosen = stay_body if fits else body
        return jax.shard_map(chosen, mesh=mesh, in_specs=in_specs, out_specs=out_specs, check_vma=False)(
            hidden, gains, up_rows, down_rows, pick)

    return whole
```

```python
import functools

import jax
import jax.numpy as jnp
from jax import lax
from jax.experimental import pallas as pl
from jax.experimental.pallas import tpu as pltpu
from jax.sharding import PartitionSpec as P

BLOCK = 128
LAYERS = 2
CORES = 2
TWINS = 2
VMEM_BUDGET = 40 * 1024 * 1024
FETCH_BUDGET = 40 * 1024 * 1024
CHUNK = 1024


def sublayers_kernel(
    owners, batches,
    hidden_ref, gains_ref, live_ref, up_hbm, down_hbm, out_ref,
    state, acts, up_v, down_v, pre, pre_in, part, x_in, y_in, q_in, z_in, r_in, stat, stat_in, out_in, total, normed,
    wsem, hsem, osem, ssem, pre_sem, ag_recv, x_send, y_send, up_send, dn_send,
    rx_send, ry_send, rup_send, rdn_send, x_recv, y_recv, q_recv, z_recv, r_recv,
):
    zn = batches // CORES
    per_layer = owners // LAYERS
    rows, width = hidden_ref.shape
    half = width // CORES
    group_rows = batches * rows
    me_o = lax.axis_index("owner")
    me_b = lax.axis_index("batch")
    hi, lo = me_o // per_layer, me_o % per_layer
    zi, core = me_b // CORES, me_b % CORES
    other = 1 - core
    peer_x = hi * per_layer + (1 - lo)
    peer_y = (1 - hi) * per_layer + lo
    diag = (1 - hi) * per_layer + (1 - lo)
    x_dev, y_dev = (peer_x, me_b), (peer_y, me_b)
    p_dev = (me_o, zi * CORES + 1 - core)
    up_dev, dn_dev = (me_o, me_b + CORES), (me_o, me_b - CORES)
    has_up, has_dn = zi < zn - 1, zi > 0
    lower = zi < zn // 2
    upper = zi >= zn // 2
    low = lower.astype(jnp.int32)
    twin = zi + 1 - 2 * (zi % 2)
    inner = jnp.logical_and(zi > 0, zi < zn - 1)
    outer = jnp.logical_not(inner)
    outer_lower, outer_upper = jnp.logical_and(outer, lower), jnp.logical_and(outer, upper)
    inner_lower, inner_upper = jnp.logical_and(inner, lower), jnp.logical_and(inner, upper)
    mine = pl.ds(pl.multiple_of(core * half, 128), half)
    theirs = pl.ds(pl.multiple_of((1 - core) * half, 128), half)
    parts = range(CORES)

    def remote(src, dst, send, recv, dev):
        return pltpu.make_async_remote_copy(
            src_ref=src, dst_ref=dst, send_sem=send, recv_sem=recv,
            device_id=dev, device_id_type=pl.DeviceIdType.MESH)

    def always():
        return True

    def is_inner():
        return inner

    def is_outer():
        return outer

    def when(cond, run):
        if cond is True:
            run()
        else:
            pl.when(cond)(run)

    barrier = pltpu.get_barrier_semaphore()
    for cond, dev in ((True, x_dev), (True, y_dev), (True, p_dev), (has_up, up_dev), (has_dn, dn_dev)):
        when(cond, lambda dev=dev: pl.semaphore_signal(
            barrier, inc=1, device_id=dev, device_id_type=pl.DeviceIdType.MESH))
    normed[...] = normalize(hidden_ref[...], gains_ref[0])
    acts[0, me_o, zi, core] = normed[:, mine]
    state[core] = hidden_ref[:, mine]
    pl.semaphore_wait(barrier, 3 + has_up.astype(jnp.int32) + has_dn.astype(jnp.int32))

    swap_normed = remote(normed.at[:, theirs], acts.at[0, me_o, zi, core], hsem.at[0], hsem.at[1], p_dev)
    swap_state = remote(hidden_ref.at[:, theirs], state.at[core], hsem.at[2], hsem.at[3], p_dev)
    swap_normed.start()
    swap_state.start()

    blocks = ((up_hbm, up_v), (down_hbm, down_v))

    def keep(n, g):
        hbm, vmem = blocks[n]
        return pltpu.make_async_copy(hbm.at[g, :, mine], vmem.at[g, core], wsem.at[n, 0, g])

    def give(n, g):
        hbm, vmem = blocks[n]
        return remote(hbm.at[g, :, theirs], vmem.at[g, core], wsem.at[n, 1, g], wsem.at[n, 2, g], p_dev)

    def wait_weight(n, g):
        keep(n, g).wait()
        give(n, g).wait_recv()

    class Sender:
        def __init__(self, layer):
            self.layer, self.log = layer, []

        def go(self, src, dst, send, recv, dev, cond=always):
            when(cond(), lambda: remote(src, dst, send(self.layer), recv, dev).start())
            self.log.append((send, cond))

        def flush(self):
            for send, cond in self.log:
                when(cond(), lambda send=send: remote(
                    out_in, out_in, send(self.layer), osem.at[1], x_dev).wait_send())
            self.log.clear()

        def spread_piece(self, sems, g, j, i, slot, dev, cond):
            ref = acts.at[self.layer, g, j, i]
            self.go(ref, ref, lambda layer: sems.at[layer, slot, i], ag_recv.at[self.layer, g, j, i], dev, cond)

        def x(self, g, j, i, slot, cond=always):
            self.spread_piece(x_send, g, j, i, slot, x_dev, cond)

        def y(self, g, j, i, slot, cond=always):
            self.spread_piece(y_send, g, j, i, slot, y_dev, cond)

        def up(self, g, j, i, slot, cond):
            self.spread_piece(up_send, g, j, i, slot, up_dev, cond)

        def dn(self, g, j, i, slot, cond):
            self.spread_piece(dn_send, g, j, i, slot, dn_dev, cond)

    def arrive(layer, g, j, i):
        ref = acts.at[layer, g, j, i]
        remote(ref, ref, x_send.at[0, 0, 0], ag_recv.at[layer, g, j, i], x_dev).wait_recv()

    def below(k):
        return lambda: zi - k >= 0

    def above(k):
        return lambda: zi + k < zn

    def column(t, k, i):
        for j, there, send, more in ((zi - k, below(k), t.up, has_up), (zi + k, above(k), t.dn, has_dn)):
            when(there(), lambda j=j: arrive(t.layer, me_o, j, i))
            if k < zn - 1:
                send(me_o, j, i, k, lambda there=there, more=more: jnp.logical_and(there(), more))

    def across(send, k, i, place=always):
        send(me_o, zi - k, i, k, lambda: jnp.logical_and(below(k)(), place()))
        send(me_o, zi + k, i, zn - 1 + k, lambda: jnp.logical_and(above(k)(), place()))

    def combine(dst, terms):
        total = dst[...].astype(jnp.float32)
        for term in terms:
            total = total + term[...].astype(jnp.float32)
        dst[...] = total.astype(jnp.bfloat16)

    def line(t, col, k, i, fold):
        for j, there, slot, behind, sends, dev in (
            (zi + k, above(k), zi + k, has_dn, rup_send, up_dev),
            (zi - k, below(k), zn if k == 1 else zi - k, has_up, rdn_send, dn_dev),
        ):
            @pl.when(there())
            def _(j=j, behind=behind):
                fold(j, i, k)

                @pl.when(behind)
                def _():
                    z_wait(t.layer, j, i)
                    combine(col(j, i), [z_in.at[t.layer, j, i]])

            t.go(col(j, i), z_in.at[t.layer, slot, i], lambda layer, sends=sends: sends.at[layer, k, i],
                 z_recv.at[t.layer, slot, i], dev, there)

    def z_wait(layer, slot, i):
        ref = z_in.at[layer, slot, i]
        remote(ref, ref, rup_send.at[0, 0, 0], z_recv.at[layer, slot, i], up_dev).wait_recv()

    def home(layer, col, i, fold):
        fold(zi, i, 0)
        total[...] = state[i].astype(jnp.float32) + col(zi, i)[...].astype(jnp.float32)
        for cond, slot in ((has_dn, zi), (has_up, zn)):
            @pl.when(cond)
            def _(slot=slot):
                z_wait(layer, slot, i)
                total[...] = total[...] + z_in[layer, slot, i].astype(jnp.float32)

        state[i] = total[...].astype(jnp.bfloat16)

        @pl.when(layer < LAYERS - 1)
        def _():
            renew(layer + 1, i)

    def hidden_sum(layer, g):
        wait_weight(0, g)
        flat = acts[layer, g].reshape(group_rows, half)
        pre[g] = lax.dot_general(
            flat, up_v[g].reshape(CORES * BLOCK, half), (((1,), (1,)), ((), ())), preferred_element_type=jnp.float32)
        swap_pre(g).start()

    def swap_pre(g):
        return remote(pre.at[g], pre_in.at[g], pre_sem.at[0, g], pre_sem.at[1, g], p_dev)

    def spread(g):
        wait_weight(1, g)
        swap_pre(g).wait_recv()
        both = pre[g] + pre_in[g]
        active = (jnp.maximum(both, 0.0) * live_ref[pl.ds(g, 1), :]).astype(jnp.bfloat16)
        for at in range(0, half, CHUNK):
            cols = pl.ds(at, min(CHUNK, half - at))
            made = jnp.dot(active, down_v[g, :, :, cols].reshape(CORES * BLOCK, -1), preferred_element_type=jnp.float32)
            part[g, :, :, :, cols] = made.astype(jnp.bfloat16).reshape(zn, CORES, rows, -1)

    def middle(send, i):
        for sign, slot in ((-1, 1), (1, zn)):
            send(me_o, zi + sign, i, slot, lambda sign=sign: jnp.logical_and(inner, zi + sign != twin))

    def begin(layer, i, toward):
        ahead = Sender(layer)
        (ahead.x if toward is x_dev else ahead.y)(me_o, zi, i, 0)
        ahead.up(me_o, zi, i, 0, lambda: has_up)
        ahead.dn(me_o, zi, i, 0, lambda: has_dn)

    def ending(t, col, fold, toward):
        for i in parts:
            home(t.layer, col, i, fold)
            if i == 0:
                t.flush()

            @pl.when(t.layer < LAYERS - 1)
            def _(i=i):
                renew_done(t.layer + 1, i)
                begin(t.layer + 1, i, toward)

    def opening(t, toward, sems):
        @pl.when(t.layer == 0)
        def _():
            begin(t.layer, core, toward)
            swap_normed.wait_recv()
            begin(t.layer, other, toward)
            for n in range(len(blocks)):
                for g in range(owners):
                    keep(n, g).start()
                    give(n, g).start()
            swap_state.wait()
            swap_normed.wait_send()

        for i in parts:
            for used, cond in ((sems, always), (up_send, lambda: has_up), (dn_send, lambda: has_dn)):
                t.log.append((lambda layer, used=used, i=i: used.at[layer, 0, i], cond))

    def plane(layer):
        t = Sender(layer)
        opening(t, x_dev, x_send)
        far = [low * (zn // 2 + n) + (1 - low) * (zn // 2 - 1 - n) for n in range(zn // 2)]

        def at_inner(g, j, i):
            when(inner, lambda: arrive(layer, g, j, i))

        def at_outer(g, j, i):
            when(outer, lambda: arrive(layer, g, j, i))

        def diagonal(j, i, slot):
            at_inner(diag, j, i)
            t.up(diag, j, i, slot, lambda: inner_lower)
            t.dn(diag, j, i, slot, lambda: inner_upper)

        def relay(n, i):
            at_inner(diag, far[n], i)
            t.dn(diag, far[n], i, zn - 1 + n, lambda: inner_lower)
            t.up(diag, far[n], i, zn - 1 + n, lambda: inner_upper)

        for i in parts:
            arrive(layer, peer_y, zi, i)
            t.x(peer_y, zi, i, 2 * zn - 1, is_inner)
            at_outer(peer_x, zi, i)
            for g, slot in ((peer_y, zn - 1), (peer_x, zn)):
                t.up(g, zi, i, slot, lambda: outer_lower)
                t.dn(g, zi, i, slot, lambda: outer_upper)
            column(t, 1, i)
            across(t.x, 1, i, is_outer)
        for i in parts:
            middle(t.x, i)
        for i in parts:
            diagonal(zi, i, zn - 1)
            column(t, 2, i)
            across(t.x, 2, i)
        for i in parts:
            diagonal(twin, i, zn)
            for k in range(3, zn):
                column(t, k, i)
                across(t.x, k, i)
            relay(0, i)
        for i in parts:
            t.x(peer_y, zi, i, 2 * zn - 1, is_outer)
        hidden_sum(layer, me_o)
        for n in range(1, zn // 2):
            for i in parts:
                relay(n, i)
        spread(me_o)

        def away(k):
            return ((zi + k, above(k), k), (zi - k, below(k), zn - 1 + k))

        def give_x(g, j, i, slot, to, cond=always):
            t.go(part.at[g, j, i], x_in.at[to, i], lambda layer: rx_send.at[slot, i], x_recv.at[to, i], x_dev, cond)

        def give_y(g, j, i, slot, to, cond=always):
            t.go(part.at[g, j, i], y_in.at[to, i], lambda layer: ry_send.at[slot, i], y_recv.at[to, i], y_dev, cond)

        def relay_wait(j, i):
            ref = r_in.at[j, i]
            remote(ref, ref, rup_send.at[0, 0, 0], r_recv.at[j, i], up_dev).wait_recv()

        def relayed(j, i):
            @pl.when(inner)
            def _():
                relay_wait(j, i)
                combine(part.at[diag, j, i], [r_in.at[j, i]])

        def give_z(n, i, place):
            for sends, dev, side in ((rup_send, up_dev, lower), (rdn_send, dn_dev, upper)):
                t.go(part.at[diag, far[n], i], r_in.at[far[n], i],
                     lambda layer, sends=sends: sends.at[layer, zn + n, i],
                     r_recv.at[far[n], i], dev, lambda side=side: jnp.logical_and(side, place))

        def relay_in(n, i):
            relayed(far[n], i)
            give_z(n, i, inner)

        def col(j, i):
            return part.at[me_o, j, i]

        def x_wait(slot, i):
            ref = x_in.at[slot, i]
            remote(ref, ref, rx_send.at[0, 0], x_recv.at[slot, i], x_dev).wait_recv()

        def fold(j, i, k):
            def run():
                x_wait(j, i)
                combine(col(j, i), [x_in.at[j, i]])

            when(jnp.logical_or(outer, j != twin) if k == 1 else True, run)

        gathered, t = t, Sender(layer)

        def wait_x():
            for i in parts:
                at_inner(peer_x, zi, i)
            for k in range(1, zn):
                for j, there in ((zi - k, below(k)), (zi + k, above(k))):
                    for i in parts:
                        when(there(), lambda j=j, i=i: arrive(layer, peer_x, j, i))

        def wait_y():
            for k in range(1, zn):
                for j, there in ((zi - k, below(k)), (zi + k, above(k))):
                    for i in parts:
                        when(there(), lambda j=j, i=i: arrive(layer, peer_y, j, i))

        def wait_diag():
            for j in [zi, twin] + far:
                for i in parts:
                    arrive(layer, diag, j, i)

        def aside(k, up):
            if k > 1:
                return True
            return jnp.logical_or(outer, (zi + 1 if up else zi - 1) != twin)

        def give_twin(g, i, slot):
            for sends, dev, cond in ((rdn_send, dn_dev, inner_lower), (rup_send, up_dev, inner_upper)):
                t.go(part.at[g, twin, i], r_in.at[slot, i], lambda layer, sends=sends: sends.at[layer, zn + slot, i],
                     r_recv.at[slot, i], dev, lambda cond=cond: cond)

        def join_twin(g, i, slot):
            @pl.when(outer)
            def _():
                relay_wait(slot, i)
                combine(part.at[g, zi, i], [r_in.at[slot, i]])

        def send_x(place):
            for k in range(zn - 1, 0, -1):
                for j, there, slot in away(k):
                    for i in parts:
                        give_x(peer_x, j, i, slot, j, lambda there=there, k=k, up=slot == k: (
                            jnp.logical_and(jnp.logical_and(there(), place), aside(k, up))))

        def send_y(place):
            for k in range(zn - 1, 1, -1):
                for j, there, slot in away(k):
                    for i in parts:
                        give_y(peer_y, j, i, slot, j, lambda there=there: jnp.logical_and(there(), place))

        inside = inner.astype(jnp.int32)

        def either(at_in, at_out):
            return inside * at_in + (1 - inside) * at_out

        when(outer, wait_x)
        hidden_sum(layer, either(diag, peer_x))
        when(inner, wait_x)
        when(outer, wait_y)
        hidden_sum(layer, either(peer_x, peer_y))
        when(outer, lambda: spread(peer_x))
        send_x(outer)
        when(outer, lambda: spread(peer_y))
        send_y(outer)
        when(outer, wait_diag)
        when(inner, wait_y)
        hidden_sum(layer, either(peer_y, diag))
        when(inner, lambda: spread(peer_x))
        send_x(inner)
        when(inner, lambda: spread(peer_y))
        send_y(inner)
        for i in parts:
            give_y(peer_y, 2 * zi - twin, i, 1, 2 * zi - twin, lambda: inner)
        for i in parts:
            give_twin(peer_x, i, 0)
            give_twin(peer_y, i, 1)
        spread(diag)
        for n in reversed(range(zn // 2)):
            for i in parts:
                give_z(n, i, outer)
        gathered.flush()
        for g in range(owners):
            swap_pre(g).wait_send()
            for n in range(len(blocks)):
                give(n, g).wait_send()
        for n in reversed(range(1, zn // 2)):
            for i in parts:
                relay_in(n, i)
        for i in parts:
            relay_in(0, i)
            for k in range(zn - 1, 2, -1):
                line(t, col, k, i, fold)
            relayed(twin, i)
            give_y(diag, twin, i, 2 * zn - 1, zn)
        for i in parts:
            give_y(peer_y, twin, i, zn, twin, is_outer)
        for i in parts:
            relayed(zi, i)
            give_x(diag, zi, i, 2 * zn - 1, zn)
            line(t, col, 2, i, fold)
        for i in parts:
            join_twin(peer_x, i, 0)
            give_x(peer_x, zi, i, 0, zi)
        for i in parts:
            line(t, col, 1, i, fold)
            x_wait(zn, i)
            combine(part.at[peer_y, zi, i], [x_in.at[zn, i]])
            join_twin(peer_y, i, 1)
            give_y(peer_y, zi, i, 0, zi)
        ending(t, col, fold, y_dev)

    def beside(layer):
        t = Sender(layer)
        opening(t, y_dev, y_send)

        def near(send, i):
            for sign, slot in ((-1, 1), (1, zn)):
                send(me_o, zi + sign, i, slot, lambda sign=sign: zi + sign == twin)

        for i in parts:
            column(t, 1, i)
            near(t.x, i)
            across(t.y, 1, i, is_outer)
            middle(t.y, i)
        for i in parts:
            when(inner, lambda i=i: arrive(layer, peer_x, twin, i))
            t.y(peer_x, twin, i, 2 * zn - 1, is_inner)
            column(t, 2, i)
            across(t.y, 2, i, is_outer)
        for i in parts:
            across(t.y, 2, i, is_inner)
        for k in range(3, zn):
            for i in parts:
                column(t, k, i)
                across(t.y, k, i)
        for i in parts:
            when(outer, lambda i=i: arrive(layer, peer_x, twin, i))
            t.y(peer_x, twin, i, 2 * zn - 1, is_outer)

        t.flush()

        def col(j, i):
            return y_in.at[j, i]

        def y_wait(slot, i):
            ref = y_in.at[slot, i]
            remote(ref, ref, ry_send.at[0, 0], y_recv.at[slot, i], y_dev).wait_recv()

        def fold(j, i, k):
            if k != 1:
                y_wait(j, i)
                return
            when(jnp.logical_or(outer, j != twin), lambda: y_wait(j, i))

            @pl.when(j == twin)
            def _():
                remote(q_in.at[i], q_in.at[i], rx_send.at[2 * zn, i], q_recv.at[i], x_dev).wait_recv()
                when(outer, lambda: combine(col(j, i), [q_in.at[i]]))

                @pl.when(inner)
                def _():
                    y_in[j, i] = q_in[i]

        for k in range(zn - 1, 1, -1):
            for i in parts:
                line(t, col, k, i, fold)
        for i in parts:
            y_wait(zn, i)
            t.go(y_in.at[zn, i], q_in.at[i], lambda layer, i=i: rx_send.at[2 * zn, i], q_recv.at[i], x_dev)
        for i in parts:
            line(t, col, 1, i, fold)
        ending(t, col, fold, x_dev)

    def swap_stat(layer, i):
        return remote(stat.at[layer, i], stat_in.at[layer, i], ssem.at[0, layer, i], ssem.at[1, layer, i], p_dev)

    def renew(layer, i):
        values = state[i].astype(jnp.float32)
        mean = jnp.sum(values, axis=1, keepdims=True) / half
        centered = values - mean
        stat[layer, i, 0] = jnp.broadcast_to(mean, (rows, BLOCK))
        stat[layer, i, 1] = jnp.broadcast_to(jnp.sum(centered * centered, axis=1, keepdims=True), (rows, BLOCK))
        swap_stat(layer, i).start()

    def renew_done(layer, i):
        swap_stat(layer, i).wait()
        mean, other_mean = stat[layer, i, 0][:, :1], stat_in[layer, i, 0][:, :1]
        apart = mean - other_mean
        var = (stat[layer, i, 1][:, :1] + stat_in[layer, i, 1][:, :1] + apart * apart * (half / 2)) / width
        acts[layer, me_o, zi, i] = (
            (state[i].astype(jnp.float32) - (mean + other_mean) * 0.5) * lax.rsqrt(var + 1e-05)
            * gains_ref[pl.ds(layer, 1), mine]).astype(jnp.bfloat16)

    def sublayer(layer, carry):
        @pl.when(hi == layer)
        def _():
            plane(layer)

        @pl.when(hi != layer)
        def _():
            beside(layer)

        return carry

    lax.fori_loop(0, LAYERS, sublayer, 0)

    last = remote(state.at[1 - core], out_in, osem.at[0], osem.at[1], p_dev)
    last.start()
    out_ref[:, mine] = state[core]
    last.wait()
    out_ref[:, theirs] = out_in[...]


def scratch_plan(owners, batches, rows, width):
    zn = batches // CORES
    half = width // CORES
    bf, full = jnp.bfloat16, jnp.float32
    shard = (CORES, rows, half)
    return [
        (shard, bf),
        ((LAYERS, owners, zn) + shard, bf),
        ((owners, CORES, BLOCK, half), bf),
        ((owners, CORES, BLOCK, half), bf),
        ((owners, batches * rows, CORES * BLOCK), full),
        ((owners, batches * rows, CORES * BLOCK), full),
        ((owners, zn) + shard, bf),
        ((zn + 1,) + shard, bf),
        ((zn + 1,) + shard, bf),
        (shard, bf),
        ((LAYERS, zn + 1) + shard, bf),
        ((zn,) + shard, bf),
        ((LAYERS, CORES, 2, rows, BLOCK), full),
        ((LAYERS, CORES, 2, rows, BLOCK), full),
        ((rows, half), bf),
        ((rows, half), full),
        ((rows, width), bf),
    ]


def scratch_bytes(plan):
    total = 0
    for shape, kind in plan:
        size = jnp.dtype(kind).itemsize
        for extent in shape:
            size *= extent
        total += size
    return total


def run_sublayers(owners, batches, hidden, gains, live, up_send, down_send):
    rows, width = hidden.shape
    zn = batches // CORES
    plan = scratch_plan(owners, batches, rows, width)
    dma = pltpu.SemaphoreType.DMA
    sems = [
        (2, 3, owners), (4,), (2,), (2, LAYERS, CORES), (2, owners), (LAYERS, owners, zn, CORES),
        (LAYERS, 2 * zn, CORES), (LAYERS, 2 * zn, CORES), (LAYERS, 2 * zn, CORES), (LAYERS, 2 * zn, CORES),
        (2 * zn + 1, CORES), (2 * zn, CORES), (LAYERS, 2 * zn, CORES), (LAYERS, 2 * zn, CORES),
        (zn + 1, CORES), (zn + 1, CORES), (CORES,), (LAYERS, zn + 1, CORES), (zn, CORES),
    ]
    vmem = pl.BlockSpec(memory_space=pltpu.VMEM)
    hbm = pl.BlockSpec(memory_space=pl.ANY)
    return pl.pallas_call(
        functools.partial(sublayers_kernel, owners, batches),
        out_shape=jax.ShapeDtypeStruct((rows, width), jnp.bfloat16),
        in_specs=[vmem] * 5,
        out_specs=vmem,
        scratch_shapes=[pltpu.VMEM(s, d) for s, d in plan] + [dma(s) for s in sems],
        compiler_params=pltpu.CompilerParams(
            collective_id=0, has_side_effects=True, vmem_limit_bytes=VMEM_BUDGET),
        name="sublayers",
    )(hidden, gains, live, up_send, down_send)


def fetch_kernel(owners, batches, held, pick_ref, up_ref, down_ref, live_ref, up_out, down_out, sem):
    sender = lax.axis_index("owner") * batches + lax.axis_index("batch")

    unit = lax.broadcasted_iota(jnp.int32, (1, pick_ref.shape[1]), 1)

    def picked(g, at):
        return jnp.sum(jnp.where(unit == at, pick_ref[g:g + 1, :], 0))

    chosen = [jnp.minimum(picked(g, sender), held - 1) for g in range(owners)]

    def read(i):
        g = i % owners
        src, dst = (up_ref, up_out) if i < owners else (down_ref, down_out)
        return pltpu.make_async_copy(src.at[chosen[g]], dst.at[g], sem.at[i])

    copies = [read(i) for i in range(2 * owners)]
    for copy in copies:
        copy.start()
    first = sender - sender % CORES
    for g in range(owners):
        for n in range(CORES):
            live = (picked(g, first + n) < held).astype(jnp.float32)
            live_ref[g:g + 1, n * BLOCK:(n + 1) * BLOCK] = jnp.full((1, BLOCK), live, jnp.float32)
    for copy in copies:
        copy.wait()


def fetch(owners, batches, up_rows, down_rows, pick, near):
    width = up_rows.shape[1]
    held = up_rows.shape[0] // BLOCK
    hbm = pl.BlockSpec(memory_space=pl.ANY)
    vmem = pl.BlockSpec(memory_space=pltpu.VMEM)
    shape = (owners, BLOCK, width)
    sent = pltpu.VMEM(shape, up_rows.dtype) if near else jax.ShapeDtypeStruct(shape, up_rows.dtype)
    return pl.pallas_call(
        functools.partial(fetch_kernel, owners, batches, held),
        out_shape=(jax.ShapeDtypeStruct((owners, CORES * BLOCK), jnp.float32), sent, sent),
        in_specs=[vmem, hbm, hbm],
        out_specs=(vmem, vmem, vmem) if near else (vmem, hbm, hbm),
        scratch_shapes=[pltpu.SemaphoreType.DMA((2 * owners,))],
        compiler_params=pltpu.CompilerParams(vmem_limit_bytes=FETCH_BUDGET),
        name="fetch",
    )(pick, up_rows.reshape(held, BLOCK, width), down_rows.reshape(held, BLOCK, width))


def stay_body(hidden, gains, up_rows, down_rows, pick):
    owners = lax.axis_size("owner")
    batches = lax.axis_size("batch")
    live, up_send, down_send = fetch(owners, batches, up_rows, down_rows, pick, True)
    return run_sublayers(owners, batches, hidden, gains, live, up_send, down_send)


def normalize(rows_in, gain_row):
    values = rows_in.astype(jnp.float32)
    row_mean = jnp.mean(values, axis=1, keepdims=True)
    centered = values - row_mean
    row_var = jnp.mean(centered * centered, axis=1, keepdims=True)
    return (centered * lax.rsqrt(row_var + 1e-05) * gain_row[None, :]).astype(jnp.bfloat16)


def body(hidden, gains, up_rows, down_rows, pick):
    owners = lax.axis_size("owner")
    batches = lax.axis_size("batch")
    group_at = lax.axis_index("owner")
    lane_at = lax.axis_index("batch")
    held_blocks = up_rows.shape[0] // BLOCK
    model_width = up_rows.shape[1]
    local_rows = hidden.shape[0]
    _, up_send, down_send = fetch(owners, batches, up_rows, down_rows, pick, False)
    group_picks = lax.dynamic_slice_in_dim(pick, group_at, 1, 0)[0]
    live_slots = (group_picks[jnp.arange(owners) * batches + lane_at] < held_blocks).astype(
        jnp.float32
    )
    up_recv, down_recv = (
        lax.all_to_all(up_send, "owner", split_axis=0, concat_axis=0, tiled=True),
        lax.all_to_all(down_send, "owner", split_axis=0, concat_axis=0, tiled=True),
    )
    per_layer = owners // LAYERS
    residual = hidden
    for layer_at in range(LAYERS):
        first_slot = layer_at * per_layer
        up_part = up_recv[first_slot : first_slot + per_layer]
        down_part = down_recv[first_slot : first_slot + per_layer]
        keep_slots = live_slots[first_slot : first_slot + per_layer]
        up_flat = up_part.reshape(per_layer * BLOCK, model_width)
        down_flat = down_part.reshape(per_layer * BLOCK, model_width)
        neuron_mask = jnp.repeat(keep_slots, BLOCK)
        normed = normalize(residual, gains[layer_at])

        def expand(
            rows_piece,
            row_start,
            up_part=up_part,
            up_flat=up_flat,
            keep_slots=keep_slots,
            neuron_mask=neuron_mask,
        ):
            pre_act = lax.dot_general(
                rows_piece, up_flat, (((1,), (1,)), ((), ())), preferred_element_type=jnp.float32
            )
            return (jnp.maximum(pre_act, 0.0) * neuron_mask[None, :]).astype(jnp.bfloat16)

        active = expand(lax.all_gather(normed, "batch", axis=0, tiled=True), jnp.int32(0))

        def contract(
            row_start,
            row_count,
            active=active,
            down_part=down_part,
            down_flat=down_flat,
            keep_slots=keep_slots,
        ):
            return jnp.dot(active, down_flat, preferred_element_type=jnp.float32)

        summed = lax.psum_scatter(
            contract(jnp.int32(0), lax.axis_size("batch") * local_rows).astype(jnp.bfloat16),
            "batch",
            scatter_dimension=0,
            tiled=True,
        ).astype(jnp.float32)
        residual = (residual.astype(jnp.float32) + summed).astype(jnp.bfloat16)
    return residual


def solution(mesh):
    in_specs = (
        P(("owner", "batch"), None),
        P(),
        P(("owner", "batch"), None),
        P(("owner", "batch"), None),
        P(),
    )
    out_specs = P(("owner", "batch"), None)
    owners, batches = mesh.shape["owner"], mesh.shape["batch"]

    def whole(hidden, gains, up_rows, down_rows, pick):
        rows = hidden.shape[0] // (owners * batches)
        plan = scratch_plan(owners, batches, rows, hidden.shape[1])
        line = batches == 2 * TWINS * CORES
        fits = line and owners == 2 * LAYERS and scratch_bytes(plan) * 5 < VMEM_BUDGET * 4
        chosen = stay_body if fits else body
        return jax.shard_map(chosen, mesh=mesh, in_specs=in_specs, out_specs=out_specs, check_vma=False)(
            hidden, gains, up_rows, down_rows, pick)

    return whole
```

```python
import functools

import jax
import jax.numpy as jnp
from jax import lax
from jax.experimental import pallas as pl
from jax.experimental.pallas import tpu as pltpu
from jax.sharding import PartitionSpec as P

BLOCK = 128
LAYERS = 2
CORES = 2
TWINS = 2
VMEM_BUDGET = 40 * 1024 * 1024
FETCH_BUDGET = 40 * 1024 * 1024
CHUNK = 1024


def sublayers_kernel(
    owners, batches,
    hidden_ref, gains_ref, live_ref, up_hbm, down_hbm, out_ref,
    state, acts, up_v, down_v, pre, pre_in, part, x_in, y_in, q_in, z_in, r_in, stat, stat_in, out_in, total, normed,
    wsem, hsem, osem, ssem, pre_sem, ag_recv, x_send, y_send, up_send, dn_send,
    rx_send, ry_send, rup_send, rdn_send, x_recv, y_recv, q_recv, z_recv, r_recv,
):
    zn = batches // CORES
    per_layer = owners // LAYERS
    rows, width = hidden_ref.shape
    half = width // CORES
    group_rows = batches * rows
    me_o = lax.axis_index("owner")
    me_b = lax.axis_index("batch")
    hi, lo = me_o // per_layer, me_o % per_layer
    zi, core = me_b // CORES, me_b % CORES
    other = 1 - core
    peer_x = hi * per_layer + (1 - lo)
    peer_y = (1 - hi) * per_layer + lo
    diag = (1 - hi) * per_layer + (1 - lo)
    x_dev, y_dev = (peer_x, me_b), (peer_y, me_b)
    p_dev = (me_o, zi * CORES + 1 - core)
    up_dev, dn_dev = (me_o, me_b + CORES), (me_o, me_b - CORES)
    has_up, has_dn = zi < zn - 1, zi > 0
    lower = zi < zn // 2
    upper = zi >= zn // 2
    low = lower.astype(jnp.int32)
    twin = zi + 1 - 2 * (zi % 2)
    inner = jnp.logical_and(zi > 0, zi < zn - 1)
    outer = jnp.logical_not(inner)
    outer_lower, outer_upper = jnp.logical_and(outer, lower), jnp.logical_and(outer, upper)
    inner_lower, inner_upper = jnp.logical_and(inner, lower), jnp.logical_and(inner, upper)
    mine = pl.ds(pl.multiple_of(core * half, 128), half)
    theirs = pl.ds(pl.multiple_of((1 - core) * half, 128), half)
    parts = range(CORES)

    def remote(src, dst, send, recv, dev):
        return pltpu.make_async_remote_copy(
            src_ref=src, dst_ref=dst, send_sem=send, recv_sem=recv,
            device_id=dev, device_id_type=pl.DeviceIdType.MESH)

    def always():
        return True

    def is_inner():
        return inner

    def is_outer():
        return outer

    def when(cond, run):
        if cond is True:
            run()
        else:
            pl.when(cond)(run)

    barrier = pltpu.get_barrier_semaphore()
    for cond, dev in ((True, x_dev), (True, y_dev), (True, p_dev), (has_up, up_dev), (has_dn, dn_dev)):
        when(cond, lambda dev=dev: pl.semaphore_signal(
            barrier, inc=1, device_id=dev, device_id_type=pl.DeviceIdType.MESH))
    normed[...] = normalize(hidden_ref[...], gains_ref[0])
    acts[0, me_o, zi, core] = normed[:, mine]
    state[core] = hidden_ref[:, mine]
    pl.semaphore_wait(barrier, 3 + has_up.astype(jnp.int32) + has_dn.astype(jnp.int32))

    swap_normed = remote(normed.at[:, theirs], acts.at[0, me_o, zi, core], hsem.at[0], hsem.at[1], p_dev)
    swap_state = remote(hidden_ref.at[:, theirs], state.at[core], hsem.at[2], hsem.at[3], p_dev)
    swap_normed.start()
    swap_state.start()

    blocks = ((up_hbm, up_v), (down_hbm, down_v))

    def keep(n, g):
        hbm, vmem = blocks[n]
        return pltpu.make_async_copy(hbm.at[g, :, mine], vmem.at[g, core], wsem.at[n, 0, g])

    def give(n, g):
        hbm, vmem = blocks[n]
        return remote(hbm.at[g, :, theirs], vmem.at[g, core], wsem.at[n, 1, g], wsem.at[n, 2, g], p_dev)

    def wait_weight(n, g):
        keep(n, g).wait()
        give(n, g).wait_recv()

    class Sender:
        def __init__(self, layer):
            self.layer, self.log = layer, []

        def go(self, src, dst, send, recv, dev, cond=always):
            when(cond(), lambda: remote(src, dst, send(self.layer), recv, dev).start())
            self.log.append((send, cond))

        def flush(self):
            for send, cond in self.log:
                when(cond(), lambda send=send: remote(
                    out_in, out_in, send(self.layer), osem.at[1], x_dev).wait_send())

        def spread_piece(self, sems, g, j, i, slot, dev, cond):
            ref = acts.at[self.layer, g, j, i]
            self.go(ref, ref, lambda layer: sems.at[layer, slot, i], ag_recv.at[self.layer, g, j, i], dev, cond)

        def x(self, g, j, i, slot, cond=always):
            self.spread_piece(x_send, g, j, i, slot, x_dev, cond)

        def y(self, g, j, i, slot, cond=always):
            self.spread_piece(y_send, g, j, i, slot, y_dev, cond)

        def up(self, g, j, i, slot, cond):
            self.spread_piece(up_send, g, j, i, slot, up_dev, cond)

        def dn(self, g, j, i, slot, cond):
            self.spread_piece(dn_send, g, j, i, slot, dn_dev, cond)

    def arrive(layer, g, j, i):
        ref = acts.at[layer, g, j, i]
        remote(ref, ref, x_send.at[0, 0, 0], ag_recv.at[layer, g, j, i], x_dev).wait_recv()

    def below(k):
        return lambda: zi - k >= 0

    def above(k):
        return lambda: zi + k < zn

    def column(t, k, i):
        for j, there, send, more in ((zi - k, below(k), t.up, has_up), (zi + k, above(k), t.dn, has_dn)):
            when(there(), lambda j=j: arrive(t.layer, me_o, j, i))
            if k < zn - 1:
                send(me_o, j, i, k, lambda there=there, more=more: jnp.logical_and(there(), more))

    def across(send, k, i, place=always):
        send(me_o, zi - k, i, k, lambda: jnp.logical_and(below(k)(), place()))
        send(me_o, zi + k, i, zn - 1 + k, lambda: jnp.logical_and(above(k)(), place()))

    def combine(dst, terms):
        total = dst[...].astype(jnp.float32)
        for term in terms:
            total = total + term[...].astype(jnp.float32)
        dst[...] = total.astype(jnp.bfloat16)

    def line(t, col, k, i, fold):
        for j, there, slot, behind, sends, dev in (
            (zi + k, above(k), zi + k, has_dn, rup_send, up_dev),
            (zi - k, below(k), zn if k == 1 else zi - k, has_up, rdn_send, dn_dev),
        ):
            @pl.when(there())
            def _(j=j, behind=behind):
                fold(j, i, k)

                @pl.when(behind)
                def _():
                    z_wait(t.layer, j, i)
                    combine(col(j, i), [z_in.at[t.layer, j, i]])

            t.go(col(j, i), z_in.at[t.layer, slot, i], lambda layer, sends=sends: sends.at[layer, k, i],
                 z_recv.at[t.layer, slot, i], dev, there)

    def z_wait(layer, slot, i):
        ref = z_in.at[layer, slot, i]
        remote(ref, ref, rup_send.at[0, 0, 0], z_recv.at[layer, slot, i], up_dev).wait_recv()

    def home(layer, col, i, fold):
        fold(zi, i, 0)
        total[...] = state[i].astype(jnp.float32) + col(zi, i)[...].astype(jnp.float32)
        for cond, slot in ((has_dn, zi), (has_up, zn)):
            @pl.when(cond)
            def _(slot=slot):
                z_wait(layer, slot, i)
                total[...] = total[...] + z_in[layer, slot, i].astype(jnp.float32)

        state[i] = total[...].astype(jnp.bfloat16)

        @pl.when(layer < LAYERS - 1)
        def _():
            renew(layer + 1, i)

    def hidden_sum(layer, g):
        wait_weight(0, g)
        flat = acts[layer, g].reshape(group_rows, half)
        pre[g] = lax.dot_general(
            flat, up_v[g].reshape(CORES * BLOCK, half), (((1,), (1,)), ((), ())), preferred_element_type=jnp.float32)
        swap_pre(g).start()

    def swap_pre(g):
        return remote(pre.at[g], pre_in.at[g], pre_sem.at[0, g], pre_sem.at[1, g], p_dev)

    def spread(g):
        wait_weight(1, g)
        swap_pre(g).wait_recv()
        both = pre[g] + pre_in[g]
        active = (jnp.maximum(both, 0.0) * live_ref[pl.ds(g, 1), :]).astype(jnp.bfloat16)
        for at in range(0, half, CHUNK):
            cols = pl.ds(at, min(CHUNK, half - at))
            made = jnp.dot(active, down_v[g, :, :, cols].reshape(CORES * BLOCK, -1), preferred_element_type=jnp.float32)
            part[g, :, :, :, cols] = made.astype(jnp.bfloat16).reshape(zn, CORES, rows, -1)

    def middle(send, i):
        for sign, slot in ((-1, 1), (1, zn)):
            send(me_o, zi + sign, i, slot, lambda sign=sign: jnp.logical_and(inner, zi + sign != twin))

    def begin(layer, i, toward):
        ahead = Sender(layer)
        (ahead.x if toward is x_dev else ahead.y)(me_o, zi, i, 0)
        ahead.up(me_o, zi, i, 0, lambda: has_up)
        ahead.dn(me_o, zi, i, 0, lambda: has_dn)

    def ending(t, col, fold, toward):
        for i in parts:
            home(t.layer, col, i, fold)
            if i == 0:
                pl.when(t.layer == LAYERS - 1)(t.flush)

            @pl.when(t.layer < LAYERS - 1)
            def _(i=i):
                renew_done(t.layer + 1, i)
                begin(t.layer + 1, i, toward)
        pl.when(t.layer < LAYERS - 1)(t.flush)

    def opening(t, toward, sems):
        @pl.when(t.layer == 0)
        def _():
            begin(t.layer, core, toward)
            swap_normed.wait_recv()
            begin(t.layer, other, toward)
            for n in range(len(blocks)):
                for g in range(owners):
                    keep(n, g).start()
                    give(n, g).start()
            swap_state.wait()
            swap_normed.wait_send()

        for i in parts:
            for used, cond in ((sems, always), (up_send, lambda: has_up), (dn_send, lambda: has_dn)):
                t.log.append((lambda layer, used=used, i=i: used.at[layer, 0, i], cond))

    def plane(layer):
        t = Sender(layer)
        opening(t, x_dev, x_send)
        far = [low * (zn // 2 + n) + (1 - low) * (zn // 2 - 1 - n) for n in range(zn // 2)]

        def at_inner(g, j, i):
            when(inner, lambda: arrive(layer, g, j, i))

        def at_outer(g, j, i):
            when(outer, lambda: arrive(layer, g, j, i))

        def diagonal(j, i, slot):
            at_inner(diag, j, i)
            t.up(diag, j, i, slot, lambda: inner_lower)
            t.dn(diag, j, i, slot, lambda: inner_upper)

        def relay(n, i):
            at_inner(diag, far[n], i)
            t.dn(diag, far[n], i, zn - 1 + n, lambda: inner_lower)
            t.up(diag, far[n], i, zn - 1 + n, lambda: inner_upper)

        for i in parts:
            arrive(layer, peer_y, zi, i)
            t.x(peer_y, zi, i, 2 * zn - 1, is_inner)
            at_outer(peer_x, zi, i)
            for g, slot in ((peer_y, zn - 1), (peer_x, zn)):
                t.up(g, zi, i, slot, lambda: outer_lower)
                t.dn(g, zi, i, slot, lambda: outer_upper)
            column(t, 1, i)
            across(t.x, 1, i, is_outer)
        for i in parts:
            middle(t.x, i)
        for i in parts:
            diagonal(zi, i, zn - 1)
            column(t, 2, i)
            across(t.x, 2, i)
        for i in parts:
            diagonal(twin, i, zn)
            for k in range(3, zn):
                column(t, k, i)
                across(t.x, k, i)
            relay(0, i)
        for i in parts:
            t.x(peer_y, zi, i, 2 * zn - 1, is_outer)
        hidden_sum(layer, me_o)
        for n in range(1, zn // 2):
            for i in parts:
                relay(n, i)
        spread(me_o)

        def away(k):
            return ((zi + k, above(k), k), (zi - k, below(k), zn - 1 + k))

        def give_x(g, j, i, slot, to, cond=always):
            t.go(part.at[g, j, i], x_in.at[to, i], lambda layer: rx_send.at[slot, i], x_recv.at[to, i], x_dev, cond)

        def give_y(g, j, i, slot, to, cond=always):
            t.go(part.at[g, j, i], y_in.at[to, i], lambda layer: ry_send.at[slot, i], y_recv.at[to, i], y_dev, cond)

        def relay_wait(j, i):
            ref = r_in.at[j, i]
            remote(ref, ref, rup_send.at[0, 0, 0], r_recv.at[j, i], up_dev).wait_recv()

        def relayed(j, i):
            @pl.when(inner)
            def _():
                relay_wait(j, i)
                combine(part.at[diag, j, i], [r_in.at[j, i]])

        def give_z(n, i, place):
            for sends, dev, side in ((rup_send, up_dev, lower), (rdn_send, dn_dev, upper)):
                t.go(part.at[diag, far[n], i], r_in.at[far[n], i],
                     lambda layer, sends=sends: sends.at[layer, zn + n, i],
                     r_recv.at[far[n], i], dev, lambda side=side: jnp.logical_and(side, place))

        def relay_in(n, i):
            relayed(far[n], i)
            give_z(n, i, inner)

        def col(j, i):
            return part.at[me_o, j, i]

        def x_wait(slot, i):
            ref = x_in.at[slot, i]
            remote(ref, ref, rx_send.at[0, 0], x_recv.at[slot, i], x_dev).wait_recv()

        def fold(j, i, k):
            def run():
                x_wait(j, i)
                combine(col(j, i), [x_in.at[j, i]])

            when(jnp.logical_or(outer, j != twin) if k == 1 else True, run)

        gathered, t = t, Sender(layer)

        def wait_x():
            for i in parts:
                at_inner(peer_x, zi, i)
            for k in range(1, zn):
                for j, there in ((zi - k, below(k)), (zi + k, above(k))):
                    for i in parts:
                        when(there(), lambda j=j, i=i: arrive(layer, peer_x, j, i))

        def wait_y():
            for k in range(1, zn):
                for j, there in ((zi - k, below(k)), (zi + k, above(k))):
                    for i in parts:
                        when(there(), lambda j=j, i=i: arrive(layer, peer_y, j, i))

        def wait_diag():
            for j in [zi, twin] + far:
                for i in parts:
                    arrive(layer, diag, j, i)

        def aside(k, up):
            if k > 1:
                return True
            return jnp.logical_or(outer, (zi + 1 if up else zi - 1) != twin)

        def give_twin(g, i, slot):
            for sends, dev, cond in ((rdn_send, dn_dev, inner_lower), (rup_send, up_dev, inner_upper)):
                t.go(part.at[g, twin, i], r_in.at[slot, i], lambda layer, sends=sends: sends.at[layer, zn + slot, i],
                     r_recv.at[slot, i], dev, lambda cond=cond: cond)

        def join_twin(g, i, slot):
            @pl.when(outer)
            def _():
                relay_wait(slot, i)
                combine(part.at[g, zi, i], [r_in.at[slot, i]])

        def send_x(place):
            for k in range(zn - 1, 0, -1):
                for j, there, slot in away(k):
                    for i in parts:
                        give_x(peer_x, j, i, slot, j, lambda there=there, k=k, up=slot == k: (
                            jnp.logical_and(jnp.logical_and(there(), place), aside(k, up))))

        def send_y(place):
            for k in range(zn - 1, 1, -1):
                for j, there, slot in away(k):
                    for i in parts:
                        give_y(peer_y, j, i, slot, j, lambda there=there: jnp.logical_and(there(), place))

        inside = inner.astype(jnp.int32)

        def either(at_in, at_out):
            return inside * at_in + (1 - inside) * at_out

        when(outer, wait_x)
        hidden_sum(layer, either(diag, peer_x))
        when(inner, wait_x)
        when(outer, wait_y)
        hidden_sum(layer, either(peer_x, peer_y))
        when(outer, lambda: spread(peer_x))
        send_x(outer)
        when(outer, lambda: spread(peer_y))
        send_y(outer)
        when(outer, wait_diag)
        when(inner, wait_y)
        hidden_sum(layer, either(peer_y, diag))
        when(inner, lambda: spread(peer_x))
        send_x(inner)
        when(inner, lambda: spread(peer_y))
        send_y(inner)
        for i in parts:
            give_y(peer_y, 2 * zi - twin, i, 1, 2 * zi - twin, lambda: inner)
        for i in parts:
            give_twin(peer_x, i, 0)
            give_twin(peer_y, i, 1)
        spread(diag)
        for n in reversed(range(zn // 2)):
            for i in parts:
                give_z(n, i, outer)
        gathered.flush()
        for g in range(owners):
            swap_pre(g).wait_send()
            for n in range(len(blocks)):
                give(n, g).wait_send()
        for n in reversed(range(1, zn // 2)):
            for i in parts:
                relay_in(n, i)
        for i in parts:
            relay_in(0, i)
            for k in range(zn - 1, 2, -1):
                line(t, col, k, i, fold)
            relayed(twin, i)
            give_y(diag, twin, i, 2 * zn - 1, zn)
        for i in parts:
            give_y(peer_y, twin, i, zn, twin, is_outer)
        for i in parts:
            relayed(zi, i)
            give_x(diag, zi, i, 2 * zn - 1, zn)
            line(t, col, 2, i, fold)
        for i in parts:
            join_twin(peer_x, i, 0)
            give_x(peer_x, zi, i, 0, zi)
        for i in parts:
            line(t, col, 1, i, fold)
            x_wait(zn, i)
            combine(part.at[peer_y, zi, i], [x_in.at[zn, i]])
            join_twin(peer_y, i, 1)
            give_y(peer_y, zi, i, 0, zi)
        ending(t, col, fold, y_dev)

    def beside(layer):
        t = Sender(layer)
        opening(t, y_dev, y_send)

        def near(send, i):
            for sign, slot in ((-1, 1), (1, zn)):
                send(me_o, zi + sign, i, slot, lambda sign=sign: zi + sign == twin)

        for i in parts:
            column(t, 1, i)
            near(t.x, i)
            across(t.y, 1, i, is_outer)
            middle(t.y, i)
        for i in parts:
            when(inner, lambda i=i: arrive(layer, peer_x, twin, i))
            t.y(peer_x, twin, i, 2 * zn - 1, is_inner)
            column(t, 2, i)
            across(t.y, 2, i, is_outer)
        for i in parts:
            across(t.y, 2, i, is_inner)
        for k in range(3, zn):
            for i in parts:
                column(t, k, i)
                across(t.y, k, i)
        for i in parts:
            when(outer, lambda i=i: arrive(layer, peer_x, twin, i))
            t.y(peer_x, twin, i, 2 * zn - 1, is_outer)

        t.flush()
        t = Sender(layer)

        def col(j, i):
            return y_in.at[j, i]

        def y_wait(slot, i):
            ref = y_in.at[slot, i]
            remote(ref, ref, ry_send.at[0, 0], y_recv.at[slot, i], y_dev).wait_recv()

        def fold(j, i, k):
            if k != 1:
                y_wait(j, i)
                return
            when(jnp.logical_or(outer, j != twin), lambda: y_wait(j, i))

            @pl.when(j == twin)
            def _():
                remote(q_in.at[i], q_in.at[i], rx_send.at[2 * zn, i], q_recv.at[i], x_dev).wait_recv()
                when(outer, lambda: combine(col(j, i), [q_in.at[i]]))

                @pl.when(inner)
                def _():
                    y_in[j, i] = q_in[i]

        for k in range(zn - 1, 1, -1):
            for i in parts:
                line(t, col, k, i, fold)
        for i in parts:
            y_wait(zn, i)
            t.go(y_in.at[zn, i], q_in.at[i], lambda layer, i=i: rx_send.at[2 * zn, i], q_recv.at[i], x_dev)
        for i in parts:
            line(t, col, 1, i, fold)
        ending(t, col, fold, x_dev)

    def swap_stat(layer, i):
        return remote(stat.at[layer, i], stat_in.at[layer, i], ssem.at[0, layer, i], ssem.at[1, layer, i], p_dev)

    def renew(layer, i):
        values = state[i].astype(jnp.float32)
        mean = jnp.sum(values, axis=1, keepdims=True) / half
        centered = values - mean
        stat[layer, i, 0] = jnp.broadcast_to(mean, (rows, BLOCK))
        stat[layer, i, 1] = jnp.broadcast_to(jnp.sum(centered * centered, axis=1, keepdims=True), (rows, BLOCK))
        swap_stat(layer, i).start()

    def renew_done(layer, i):
        swap_stat(layer, i).wait()
        mean, other_mean = stat[layer, i, 0][:, :1], stat_in[layer, i, 0][:, :1]
        apart = mean - other_mean
        var = (stat[layer, i, 1][:, :1] + stat_in[layer, i, 1][:, :1] + apart * apart * (half / 2)) / width
        acts[layer, me_o, zi, i] = (
            (state[i].astype(jnp.float32) - (mean + other_mean) * 0.5) * lax.rsqrt(var + 1e-05)
            * gains_ref[pl.ds(layer, 1), mine]).astype(jnp.bfloat16)

    def sublayer(layer, carry):
        @pl.when(hi == layer)
        def _():
            plane(layer)

        @pl.when(hi != layer)
        def _():
            beside(layer)

        return carry

    lax.fori_loop(0, LAYERS, sublayer, 0)

    last = remote(state.at[1 - core], out_in, osem.at[0], osem.at[1], p_dev)
    last.start()
    out_ref[:, mine] = state[core]
    last.wait()
    out_ref[:, theirs] = out_in[...]


def scratch_plan(owners, batches, rows, width):
    zn = batches // CORES
    half = width // CORES
    bf, full = jnp.bfloat16, jnp.float32
    shard = (CORES, rows, half)
    return [
        (shard, bf),
        ((LAYERS, owners, zn) + shard, bf),
        ((owners, CORES, BLOCK, half), bf),
        ((owners, CORES, BLOCK, half), bf),
        ((owners, batches * rows, CORES * BLOCK), full),
        ((owners, batches * rows, CORES * BLOCK), full),
        ((owners, zn) + shard, bf),
        ((zn + 1,) + shard, bf),
        ((zn + 1,) + shard, bf),
        (shard, bf),
        ((LAYERS, zn + 1) + shard, bf),
        ((zn,) + shard, bf),
        ((LAYERS, CORES, 2, rows, BLOCK), full),
        ((LAYERS, CORES, 2, rows, BLOCK), full),
        ((rows, half), bf),
        ((rows, half), full),
        ((rows, width), bf),
    ]


def scratch_bytes(plan):
    total = 0
    for shape, kind in plan:
        size = jnp.dtype(kind).itemsize
        for extent in shape:
            size *= extent
        total += size
    return total


def run_sublayers(owners, batches, hidden, gains, live, up_send, down_send):
    rows, width = hidden.shape
    zn = batches // CORES
    plan = scratch_plan(owners, batches, rows, width)
    dma = pltpu.SemaphoreType.DMA
    sems = [
        (2, 3, owners), (4,), (2,), (2, LAYERS, CORES), (2, owners), (LAYERS, owners, zn, CORES),
        (LAYERS, 2 * zn, CORES), (LAYERS, 2 * zn, CORES), (LAYERS, 2 * zn, CORES), (LAYERS, 2 * zn, CORES),
        (2 * zn + 1, CORES), (2 * zn, CORES), (LAYERS, 2 * zn, CORES), (LAYERS, 2 * zn, CORES),
        (zn + 1, CORES), (zn + 1, CORES), (CORES,), (LAYERS, zn + 1, CORES), (zn, CORES),
    ]
    vmem = pl.BlockSpec(memory_space=pltpu.VMEM)
    hbm = pl.BlockSpec(memory_space=pl.ANY)
    return pl.pallas_call(
        functools.partial(sublayers_kernel, owners, batches),
        out_shape=jax.ShapeDtypeStruct((rows, width), jnp.bfloat16),
        in_specs=[vmem] * 5,
        out_specs=vmem,
        scratch_shapes=[pltpu.VMEM(s, d) for s, d in plan] + [dma(s) for s in sems],
        compiler_params=pltpu.CompilerParams(
            collective_id=0, has_side_effects=True, vmem_limit_bytes=VMEM_BUDGET),
        name="sublayers",
    )(hidden, gains, live, up_send, down_send)


def fetch_kernel(owners, batches, held, pick_ref, up_ref, down_ref, live_ref, up_out, down_out, sem):
    sender = lax.axis_index("owner") * batches + lax.axis_index("batch")

    unit = lax.broadcasted_iota(jnp.int32, (1, pick_ref.shape[1]), 1)

    def picked(g, at):
        return jnp.sum(jnp.where(unit == at, pick_ref[g:g + 1, :], 0))

    chosen = [jnp.minimum(picked(g, sender), held - 1) for g in range(owners)]

    def read(i):
        g = i % owners
        src, dst = (up_ref, up_out) if i < owners else (down_ref, down_out)
        return pltpu.make_async_copy(src.at[chosen[g]], dst.at[g], sem.at[i])

    copies = [read(i) for i in range(2 * owners)]
    for copy in copies:
        copy.start()
    first = sender - sender % CORES
    for g in range(owners):
        for n in range(CORES):
            live = (picked(g, first + n) < held).astype(jnp.float32)
            live_ref[g:g + 1, n * BLOCK:(n + 1) * BLOCK] = jnp.full((1, BLOCK), live, jnp.float32)
    for copy in copies:
        copy.wait()


def fetch(owners, batches, up_rows, down_rows, pick, near):
    width = up_rows.shape[1]
    held = up_rows.shape[0] // BLOCK
    hbm = pl.BlockSpec(memory_space=pl.ANY)
    vmem = pl.BlockSpec(memory_space=pltpu.VMEM)
    shape = (owners, BLOCK, width)
    sent = pltpu.VMEM(shape, up_rows.dtype) if near else jax.ShapeDtypeStruct(shape, up_rows.dtype)
    return pl.pallas_call(
        functools.partial(fetch_kernel, owners, batches, held),
        out_shape=(jax.ShapeDtypeStruct((owners, CORES * BLOCK), jnp.float32), sent, sent),
        in_specs=[vmem, hbm, hbm],
        out_specs=(vmem, vmem, vmem) if near else (vmem, hbm, hbm),
        scratch_shapes=[pltpu.SemaphoreType.DMA((2 * owners,))],
        compiler_params=pltpu.CompilerParams(vmem_limit_bytes=FETCH_BUDGET),
        name="fetch",
    )(pick, up_rows.reshape(held, BLOCK, width), down_rows.reshape(held, BLOCK, width))


def stay_body(hidden, gains, up_rows, down_rows, pick):
    owners = lax.axis_size("owner")
    batches = lax.axis_size("batch")
    live, up_send, down_send = fetch(owners, batches, up_rows, down_rows, pick, True)
    return run_sublayers(owners, batches, hidden, gains, live, up_send, down_send)


def normalize(rows_in, gain_row):
    values = rows_in.astype(jnp.float32)
    row_mean = jnp.mean(values, axis=1, keepdims=True)
    centered = values - row_mean
    row_var = jnp.mean(centered * centered, axis=1, keepdims=True)
    return (centered * lax.rsqrt(row_var + 1e-05) * gain_row[None, :]).astype(jnp.bfloat16)


def body(hidden, gains, up_rows, down_rows, pick):
    owners = lax.axis_size("owner")
    batches = lax.axis_size("batch")
    group_at = lax.axis_index("owner")
    lane_at = lax.axis_index("batch")
    held_blocks = up_rows.shape[0] // BLOCK
    model_width = up_rows.shape[1]
    local_rows = hidden.shape[0]
    _, up_send, down_send = fetch(owners, batches, up_rows, down_rows, pick, False)
    group_picks = lax.dynamic_slice_in_dim(pick, group_at, 1, 0)[0]
    live_slots = (group_picks[jnp.arange(owners) * batches + lane_at] < held_blocks).astype(
        jnp.float32
    )
    up_recv, down_recv = (
        lax.all_to_all(up_send, "owner", split_axis=0, concat_axis=0, tiled=True),
        lax.all_to_all(down_send, "owner", split_axis=0, concat_axis=0, tiled=True),
    )
    per_layer = owners // LAYERS
    residual = hidden
    for layer_at in range(LAYERS):
        first_slot = layer_at * per_layer
        up_part = up_recv[first_slot : first_slot + per_layer]
        down_part = down_recv[first_slot : first_slot + per_layer]
        keep_slots = live_slots[first_slot : first_slot + per_layer]
        up_flat = up_part.reshape(per_layer * BLOCK, model_width)
        down_flat = down_part.reshape(per_layer * BLOCK, model_width)
        neuron_mask = jnp.repeat(keep_slots, BLOCK)
        normed = normalize(residual, gains[layer_at])

        def expand(
            rows_piece,
            row_start,
            up_part=up_part,
            up_flat=up_flat,
            keep_slots=keep_slots,
            neuron_mask=neuron_mask,
        ):
            pre_act = lax.dot_general(
                rows_piece, up_flat, (((1,), (1,)), ((), ())), preferred_element_type=jnp.float32
            )
            return (jnp.maximum(pre_act, 0.0) * neuron_mask[None, :]).astype(jnp.bfloat16)

        active = expand(lax.all_gather(normed, "batch", axis=0, tiled=True), jnp.int32(0))

        def contract(
            row_start,
            row_count,
            active=active,
            down_part=down_part,
            down_flat=down_flat,
            keep_slots=keep_slots,
        ):
            return jnp.dot(active, down_flat, preferred_element_type=jnp.float32)

        summed = lax.psum_scatter(
            contract(jnp.int32(0), lax.axis_size("batch") * local_rows).astype(jnp.bfloat16),
            "batch",
            scatter_dimension=0,
            tiled=True,
        ).astype(jnp.float32)
        residual = (residual.astype(jnp.float32) + summed).astype(jnp.bfloat16)
    return residual


def solution(mesh):
    in_specs = (
        P(("owner", "batch"), None),
        P(),
        P(("owner", "batch"), None),
        P(("owner", "batch"), None),
        P(),
    )
    out_specs = P(("owner", "batch"), None)
    owners, batches = mesh.shape["owner"], mesh.shape["batch"]

    def whole(hidden, gains, up_rows, down_rows, pick):
        rows = hidden.shape[0] // (owners * batches)
        plan = scratch_plan(owners, batches, rows, hidden.shape[1])
        line = batches == 2 * TWINS * CORES
        fits = line and owners == 2 * LAYERS and scratch_bytes(plan) * 5 < VMEM_BUDGET * 4
        chosen = stay_body if fits else body
        return jax.shard_map(chosen, mesh=mesh, in_specs=in_specs, out_specs=out_specs, check_vma=False)(
            hidden, gains, up_rows, down_rows, pick)

    return whole
```
